512 devices in a mesh: inp: 8 (over z_hi, y), hid: 8 (over x, core), tok: 8 (over z_lo).
Axes of the slice: x: 4, y: 4, z: 16 (z_hi: 2, z_lo: 8; z = z_hi * 8 + z_lo), core: 2. Of those that a mesh axis runs over, the one named last changes fastest.
Arguments:
- tokens: float32 [1024, 3072], P(('tok', 'hid'), 'inp'), may hold values from -6 to 6
- targets: float32 [1024, 3072], P(('tok', 'hid'), 'inp'), may hold values from -6 to 6
- sample_ids: int32 [1024], P(('tok', 'hid')), may hold values from 0 to 15, never falling along the last dimension, each value on 1 to 128 neighbouring positions
- labels: int32 [16], replicated, may hold values from 0 to 1
- utility: float32 [16], replicated, may hold values from 0.5 to 4
- ref_loss: float32 [16], replicated, may hold values from 0.9 to 1.9
- w_in: float32 [3072, 6144], P(('inp', 'tok'), 'hid'), may hold values from -0.109375 to 0.109375
- w_out: float32 [6144, 3072], P(('hid', 'tok'), 'inp'), may hold values from -0.078125 to 0.078125
- m_in: float32 [3072, 6144], P(('inp', 'tok'), 'hid'), may hold values from -6 to 6
- m_out: float32 [6144, 3072], P(('hid', 'tok'), 'inp'), may hold values from -6 to 6
- v_in: float32 [3072, 6144], P(('inp', 'tok'), 'hid'), may hold values from 0.5 to 20
- v_out: float32 [6144, 3072], P(('hid', 'tok'), 'inp'), may hold values from 0.5 to 20
- e_in: float32 [3072, 6144], P(('inp', 'tok'), 'hid'), may hold values from -0.109375 to 0.109375
- e_out: float32 [6144, 3072], P(('hid', 'tok'), 'inp'), may hold values from -0.078125 to 0.078125
Outputs:
- loss: float32 [], replicated
- new_w_in: float32 [3072, 6144], P('inp', 'hid')
- new_w_out: float32 [6144, 3072], P('hid', 'inp')
- new_m_in: float32 [3072, 6144], P(('inp', 'tok'), 'hid')
- new_m_out: float32 [6144, 3072], P(('hid', 'tok'), 'inp')
- new_v_in: float32 [3072, 6144], P(('inp', 'tok'), 'hid')
- new_v_out: float32 [6144, 3072], P(('hid', 'tok'), 'inp')
- new_e_in: float32 [3072, 6144], P(('inp', 'tok'), 'hid')
- new_e_out: float32 [6144, 3072], P(('hid', 'tok'), 'inp')
The draws below stay inside these ranges and needn't reach their ends.
Inputs may be any that keep to these rules, and one draw needn't show every extreme that they name: `sample_ids`: sample numbers never fall along the tokens; every sample has 1 to 128 tokens, one exactly that many.
All inputs are finite; a program needn't handle non-finite values.
Results may differ from the reference program's by a relative error of at most 0.00022.
Values sent between devices are 32-bit elements; how exact they have to be, the bound alone decides.
No kernel may reach another device: no remote copies, remote signals or barrier semaphores. Data moves between devices by JAX's collectives and lax.ppermute only.
A program may use at most 64 MiB of HBM per device.

```python
import math
import jax
import jax.numpy as jnp
import numpy as np
from jax import lax

D = 3072
FF = 6144
SAMPLES = 16
TOKENS = 1024


def place_ends(values, key, low, high):
    index_at = [jax.random.randint(jax.random.fold_in(key, axis), (), 0, length) for axis, length in enumerate(values.shape)]
    widest = values.shape.index(max(values.shape))
    next_to = index_at[:widest] + [(index_at[widest] + 1) % values.shape[widest]] + index_at[widest + 1:]
    return values.at[tuple(index_at)].set(low).at[tuple(next_to)].set(high)


def block_levels(own_key, shape, cuts, least, top_value):
    loudness = 1.0
    for dim, shards_of in cuts:
        heights = jax.random.uniform(jax.random.fold_in(jax.random.fold_in(own_key, 6), dim), (shards_of,), jnp.float32, least / len(cuts), top_value / len(cuts))
        loudness = loudness * jnp.repeat(jnp.exp(heights), shape[dim] // shards_of).reshape((-1,) + (1,) * (len(shape) - 1 - dim))
    return loudness


def length_profile(number_of, total, reach, skew):
    portions = [(1 << 20) // math.isqrt(rank ** skew) + 1 for rank in range(2, number_of + 1)]
    rest, given = total - reach - (number_of - 1), [1] * (number_of - 1)
    while rest > 0:
        free = [i for i in range(number_of - 1) if given[i] < reach]
        whole, budget = sum([portions[i] for i in free]), rest
        for i in free:
            addition = min(reach - given[i], max(1, budget * portions[i] // whole), rest)
            given[i] = given[i] + addition
            rest = rest - addition
    return np.array([reach] + given)


def ragged(stream_key, amount, total, limit, lean):
    if amount == 2:
        one = jax.random.randint(stream_key, (), max(1, total - limit), min(limit, total - 1) + 1)
        return jnp.stack([one, total - one])
    tallies = jnp.asarray(length_profile(amount, total, limit, lean), jnp.int32)
    pairs = (amount - 1) // 2
    giver, sink = tallies[1:1 + 2 * pairs:2], tallies[2:2 + 2 * pairs:2]
    margin = jnp.minimum(giver - 1, limit - sink)
    passed = jax.random.randint(jax.random.fold_in(stream_key, 1), (pairs,), 0, 1 << 20) % (margin + 1)
    tallies = tallies.at[1:1 + 2 * pairs:2].set(giver - passed).at[2:2 + 2 * pairs:2].set(sink + passed)
    return tallies[jax.random.permutation(jax.random.fold_in(stream_key, 2), amount)]


def noise(own_key, shape, width, limit, shards=(), held_as=jnp.bfloat16):
    values = jax.random.normal(own_key, shape, jnp.float32) * width
    if len(shards) > 0:
        values = block_levels(own_key, shape, shards, -0.22, 0.18) * values
    return jnp.clip(values, min=-limit, max=limit).astype(held_as)


def setup_inputs(seed: int = 0) -> dict:
    splits = jax.random.split(jax.random.key(seed), 15)
    tokens = noise(splits[0], (TOKENS, D), 1.0, 6.0, ((0, 64), (1, 8)), jnp.float32)
    targets = noise(splits[1], (TOKENS, D), 1.0, 6.0, ((0, 64), (1, 8)), jnp.float32)
    sample_ids = jnp.searchsorted(jnp.cumsum(ragged(splits[2], SAMPLES, TOKENS, 2 * TOKENS // SAMPLES, 0)), jnp.arange(TOKENS), side="right").astype(jnp.int32)
    labels = place_ends(jax.random.randint(splits[3], (SAMPLES,), 0, 2), jax.random.fold_in(splits[3], 1), 0, 1).astype(jnp.int32)
    utility = jnp.clip(jnp.exp(jax.random.uniform(splits[4], (SAMPLES,), jnp.float32, math.log(0.5), math.log(4.0))), 0.5, 4.0)
    ref_loss = jnp.clip(jax.random.uniform(splits[5], (SAMPLES,), jnp.float32, 0.9, 1.9), 0.9, 1.9)
    w_in = noise(splits[6], (D, FF), D ** -0.5, 0.109375, ((0, 64), (1, 8)), jnp.float32)
    w_out = noise(splits[7], (FF, D), FF ** -0.5, 0.078125, ((0, 64), (1, 8)), jnp.float32)
    m_in = noise(splits[8], (D, FF), 1.0, 6.0, ((0, 64), (1, 8)), jnp.float32)
    m_out = noise(splits[9], (FF, D), 1.0, 6.0, ((0, 64), (1, 8)), jnp.float32)
    v_in = jnp.clip(jnp.exp(math.log(20.0) - 3.6888795 * jax.random.uniform(splits[10], (D, FF), jnp.float32) ** block_levels(splits[10], (D, FF), ((0, 64), (1, 8)), -0.2, 0.2)), 0.5, 20.0)
    v_out = jnp.clip(jnp.exp(math.log(20.0) - 3.6888795 * jax.random.uniform(splits[11], (FF, D), jnp.float32) ** block_levels(splits[11], (FF, D), ((0, 64), (1, 8)), -0.2, 0.2)), 0.5, 20.0)
    e_in = noise(splits[12], (D, FF), D ** -0.5, 0.109375, ((0, 64), (1, 8)), jnp.float32)
    e_out = noise(splits[13], (FF, D), FF ** -0.5, 0.078125, ((0, 64), (1, 8)), jnp.float32)
    return {"tokens": tokens, "targets": targets, "sample_ids": sample_ids, "labels": labels, "utility": utility, "ref_loss": ref_loss, "w_in": w_in, "w_out": w_out, "m_in": m_in, "m_out": m_out, "v_in": v_in, "v_out": v_out, "e_in": e_in, "e_out": e_out}


highest = lax.Precision.HIGHEST
gelu_c = 0.7978845608028654
gelu_k = 0.044715
kto_beta = 4.0
loss_scale = 1048576.0
beta_one = 0.9
beta_two = 0.95
adam_eps = 1e-08
learn_rate = 0.001
decay_rate = 0.1
ema_rate = 0.99
bias_one = 1.0 - 0.9 ** 10
bias_two = 1.0 - 0.95 ** 10

def gelu_parts(hidden):
    inner = gelu_c * (hidden + gelu_k * hidden * hidden * hidden)
    tangent = jnp.tanh(inner)
    active = 0.5 * hidden * (1.0 + tangent)
    slope = 0.5 * (1.0 + tangent) + 0.5 * hidden * (1.0 - tangent * tangent) * gelu_c * (1.0 + 3.0 * gelu_k * hidden * hidden)
    return (active, slope)

def adamw(weight, moment_one, moment_two, average, gradient):
    moment_one = beta_one * moment_one + (1.0 - beta_one) * gradient
    moment_two = beta_two * moment_two + (1.0 - beta_two) * gradient * gradient
    update = learn_rate * (moment_one / bias_one) / (jnp.sqrt(moment_two / bias_two) + adam_eps)
    weight = weight - update - learn_rate * decay_rate * weight
    average = ema_rate * average + (1.0 - ema_rate) * weight
    return (weight, moment_one, moment_two, average)

def kto_terms(sq_sums, counts, labels, utility, ref_loss):
    sample_loss = sq_sums / (counts * D)
    signs = 2.0 * labels.astype(jnp.float32) - 1.0
    chosen = jax.nn.sigmoid(signs * kto_beta * (ref_loss - sample_loss))
    loss = -jnp.sum(utility * chosen) / SAMPLES
    dloss = utility * chosen * (1.0 - chosen) * signs * kto_beta / SAMPLES
    sample_coef = loss_scale * 2.0 * dloss / (counts * D)
    return (loss, sample_coef)

def reference(tokens, targets, sample_ids, labels, utility, ref_loss, w_in, w_out, m_in, m_out, v_in, v_out, e_in, e_out):
    hidden = jnp.dot(tokens, w_in, precision=highest, preferred_element_type=jnp.float32)
    active, slope = gelu_parts(hidden)
    output = jnp.dot(active, w_out, precision=highest, preferred_element_type=jnp.float32)
    error_rows = output - targets
    onehot = (sample_ids[:, None] == jnp.arange(SAMPLES, dtype=jnp.int32)[None, :]).astype(jnp.float32)
    token_sq = lax.optimization_barrier(jnp.sum(error_rows * error_rows, axis=1))
    sq_sums = jnp.dot(token_sq, onehot, precision=highest)
    counts = lax.optimization_barrier(jnp.sum(onehot, axis=0))
    loss, sample_coef = kto_terms(sq_sums, counts, labels, utility, ref_loss)
    d_output = error_rows * jnp.dot(onehot, sample_coef, precision=highest)[:, None]
    grad_out = lax.dot_general(active, d_output, (((0,), (0,)), ((), ())), precision=highest)
    d_active = lax.dot_general(d_output, w_out, (((1,), (1,)), ((), ())), precision=highest)
    d_hidden = d_active * slope
    grad_in = lax.dot_general(tokens, d_hidden, (((0,), (0,)), ((), ())), precision=highest)
    new_w_in, new_m_in, new_v_in, new_e_in = adamw(w_in, m_in, v_in, e_in, grad_in)
    new_w_out, new_m_out, new_v_out, new_e_out = adamw(w_out, m_out, v_out, e_out, grad_out)
    return (loss, new_w_in, new_w_out, new_m_in, new_m_out, new_v_in, new_v_out, new_e_in, new_e_out)
```

```python
import jax
import jax.numpy as jnp
from jax import lax
from jax.sharding import PartitionSpec as P

D = 3072
SAMPLES = 16


mixed = lax.Precision.HIGH
highest = lax.Precision.HIGHEST
gelu_c = 0.7978845608028654
gelu_k = 0.044715
kto_beta = 4.0
loss_scale = 1048576.0
beta_one = 0.9
beta_two = 0.95
adam_eps = 1e-08
learn_rate = 0.001
decay_rate = 0.1
ema_rate = 0.99
bias_one = 1.0 - 0.9**10
bias_two = 1.0 - 0.95**10


Y_GROUPS = [[0, 1, 2, 3], [4, 5, 6, 7]]
Z_SWAP = [(i, (i + 4) % 8) for i in range(8)]
FOLD = None


def gelu_parts(hidden):
    inner = gelu_c * (hidden + gelu_k * hidden * hidden * hidden)
    tangent = jnp.tanh(inner)
    active = 0.5 * hidden * (1.0 + tangent)
    slope = 0.5 * (1.0 + tangent) + 0.5 * hidden * (1.0 - tangent * tangent) * gelu_c * (
        1.0 + 3.0 * gelu_k * hidden * hidden
    )
    return (active, slope)


def adamw(weight, moment_one, moment_two, average, gradient):
    moment_one = beta_one * moment_one + (1.0 - beta_one) * gradient
    moment_two = beta_two * moment_two + (1.0 - beta_two) * gradient * gradient
    update = learn_rate * (moment_one / bias_one) / (jnp.sqrt(moment_two / bias_two) + adam_eps)
    weight = weight - update - learn_rate * decay_rate * weight
    average = ema_rate * average + (1.0 - ema_rate) * weight
    return (weight, moment_one, moment_two, average)


def kto_terms(sq_sums, counts, labels, utility, ref_loss):
    sample_loss = sq_sums / (counts * D)
    signs = 2.0 * labels.astype(jnp.float32) - 1.0
    chosen = jax.nn.sigmoid(signs * kto_beta * (ref_loss - sample_loss))
    loss = -jnp.sum(utility * chosen) / SAMPLES
    dloss = utility * chosen * (1.0 - chosen) * signs * kto_beta / SAMPLES
    sample_coef = loss_scale * 2.0 * dloss / (counts * D)
    return (loss, sample_coef)


def product(left, right, left_dim, right_dim):
    return lax.dot_general(
        left,
        right,
        (((left_dim,), (right_dim,)), ((), ())),
        precision=mixed,
        preferred_element_type=jnp.float32,
    )


def scatter_sum(part, axis, size, groups=None):
    blocks = part.reshape(size, part.shape[0] // size, part.shape[1])
    return jnp.sum(lax.all_to_all(blocks, axis, 0, 0, axis_index_groups=groups), axis=0)


def spread(block, axis, size, groups=None):
    copies = jnp.broadcast_to(block[None], (size,) + block.shape)
    return lax.all_to_all(copies, axis, 0, 0, axis_index_groups=groups)


def inp_sum_quarter(part):
    quarter = scatter_sum(part, "inp", 4, Y_GROUPS)
    return quarter + lax.ppermute(quarter, "inp", Z_SWAP)


def y_gather(block):
    every = spread(block, "inp", 4, Y_GROUPS)
    return every.reshape(4 * block.shape[0], block.shape[1])


def tok_gather(shard):
    return lax.all_gather(shard, "tok", axis=0, tiled=True)


def tok_scatter(full):
    return lax.psum_scatter(full, "tok", scatter_dimension=0, tiled=True)


def on_device(
    tokens,
    targets,
    sample_ids,
    labels,
    utility,
    ref_loss,
    w_in,
    w_out,
    m_in,
    m_out,
    v_in,
    v_out,
    e_in,
    e_out,
):
    w_in_block = tok_gather(w_in)
    w_out_block = tok_gather(w_out)
    all_rows = lax.all_gather(tokens, "hid", axis=0, tiled=True)
    all_ids = spread(sample_ids, "hid", 8).reshape(-1)
    onehot = (all_ids[:, None] == jnp.arange(SAMPLES, dtype=jnp.int32)[None, :]).astype(
        jnp.float32
    )
    hidden = inp_sum_quarter(product(all_rows, w_in_block, 1, 0))
    active_rows, slope_rows = gelu_parts(hidden)
    active = y_gather(active_rows)

    output = scatter_sum(product(active, w_out_block, 1, 0), "hid", 8)
    error = lax.all_gather(output - targets, "hid", axis=0, tiled=True)

    token_sq = jnp.sum(error * error, axis=1)
    local_sq = jnp.sum(token_sq[:, None] * onehot, axis=0)
    leading = lax.axis_index("inp") == 0
    local_counts = jnp.sum(onehot, axis=0) * jnp.where(leading, 1.0, 0.0)
    stats = jnp.concatenate([local_sq, local_counts, jnp.zeros((96,), jnp.float32)])[None, :]
    stats = jnp.sum(spread(stats, ("inp", "tok"), 64), axis=(0, 1))
    loss, sample_coef = kto_terms(
        stats[:SAMPLES], stats[SAMPLES : 2 * SAMPLES], labels, utility, ref_loss
    )
    coef = jnp.sum(onehot * sample_coef[None, :], axis=1)[:, None]

    d_output = error * coef
    grad_out = tok_scatter(product(active, d_output, 0, 0))
    d_active = inp_sum_quarter(product(d_output, w_out_block, 1, 1))
    d_hidden = y_gather(d_active * slope_rows)
    grad_in = tok_scatter(product(all_rows, d_hidden, 0, 0))

    weight_out, new_m_out, new_v_out, new_e_out = adamw(w_out, m_out, v_out, e_out, grad_out)
    weight_in, new_m_in, new_v_in, new_e_in = adamw(w_in, m_in, v_in, e_in, grad_in)
    new_w_out = tok_gather(weight_out)
    new_w_in = tok_gather(weight_in)
    return (
        loss,
        new_w_in,
        new_w_out,
        new_m_in,
        new_m_out,
        new_v_in,
        new_v_out,
        new_e_in,
        new_e_out,
    )


def solution(mesh):
    in_specs = (
        P(("tok", "hid"), "inp"),
        P(("tok", "hid"), "inp"),
        P(("tok", "hid")),
        P(),
        P(),
        P(),
        P(("inp", "tok"), "hid"),
        P(("hid", "tok"), "inp"),
        P(("inp", "tok"), "hid"),
        P(("hid", "tok"), "inp"),
        P(("inp", "tok"), "hid"),
        P(("hid", "tok"), "inp"),
        P(("inp", "tok"), "hid"),
        P(("hid", "tok"), "inp"),
    )
    out_specs = (
        P(),
        P("inp", "hid"),
        P("hid", "inp"),
        P(("inp", "tok"), "hid"),
        P(("hid", "tok"), "inp"),
        P(("inp", "tok"), "hid"),
        P(("hid", "tok"), "inp"),
        P(("inp", "tok"), "hid"),
        P(("hid", "tok"), "inp"),
    )
    return jax.shard_map(
        on_device, mesh=mesh, in_specs=in_specs, out_specs=out_specs, check_vma=False
    )
```

```python
import jax
import jax.numpy as jnp
from jax import lax
from jax.sharding import PartitionSpec as P

D = 3072
SAMPLES = 16


mixed = lax.Precision.HIGH
highest = lax.Precision.HIGHEST
gelu_c = 0.7978845608028654
gelu_k = 0.044715
kto_beta = 4.0
loss_scale = 1048576.0
beta_one = 0.9
beta_two = 0.95
adam_eps = 1e-08
learn_rate = 0.001
decay_rate = 0.1
ema_rate = 0.99
bias_one = 1.0 - 0.9**10
bias_two = 1.0 - 0.95**10


QUADS = [[0, 1, 2, 3], [4, 5, 6, 7]]
FAR_HALF = [(i, (i + 4) % 8) for i in range(8)]
FOLD = (0, 2, 4, 6, 7, 5, 3, 1)


def gelu_parts(hidden):
    inner = gelu_c * (hidden + gelu_k * hidden * hidden * hidden)
    tangent = jnp.tanh(inner)
    active = 0.5 * hidden * (1.0 + tangent)
    slope = 0.5 * (1.0 + tangent) + 0.5 * hidden * (1.0 - tangent * tangent) * gelu_c * (
        1.0 + 3.0 * gelu_k * hidden * hidden
    )
    return (active, slope)


def adamw(weight, moment_one, moment_two, average, gradient):
    moment_one = beta_one * moment_one + (1.0 - beta_one) * gradient
    moment_two = beta_two * moment_two + (1.0 - beta_two) * gradient * gradient
    update = learn_rate * (moment_one / bias_one) / (jnp.sqrt(moment_two / bias_two) + adam_eps)
    weight = weight - update - learn_rate * decay_rate * weight
    average = ema_rate * average + (1.0 - ema_rate) * weight
    return (weight, moment_one, moment_two, average)


def kto_terms(sq_sums, counts, labels, utility, ref_loss):
    sample_loss = sq_sums / (counts * D)
    signs = 2.0 * labels.astype(jnp.float32) - 1.0
    chosen = jax.nn.sigmoid(signs * kto_beta * (ref_loss - sample_loss))
    loss = -jnp.sum(utility * chosen) / SAMPLES
    dloss = utility * chosen * (1.0 - chosen) * signs * kto_beta / SAMPLES
    sample_coef = loss_scale * 2.0 * dloss / (counts * D)
    return (loss, sample_coef)


def product(left, right, left_dim, right_dim):
    return lax.dot_general(
        left,
        right,
        (((left_dim,), (right_dim,)), ((), ())),
        precision=mixed,
        preferred_element_type=jnp.float32,
    )


def scatter_sum(part, axis, size, groups=None):
    blocks = part.reshape(size, part.shape[0] // size, part.shape[1])
    return jnp.sum(lax.all_to_all(blocks, axis, 0, 0, axis_index_groups=groups), axis=0)


def spread(block, axis, size, groups=None):
    copies = jnp.broadcast_to(block[None], (size,) + block.shape)
    return lax.all_to_all(copies, axis, 0, 0, axis_index_groups=groups)


def y_sum(part):
    return scatter_sum(part, "inp", 4, QUADS)


def far_sum(quarter):
    return quarter + lax.ppermute(quarter, "inp", FAR_HALF)


def y_gather(block):
    every = spread(block, "inp", 4, QUADS)
    return every.reshape(4 * block.shape[0], block.shape[1])


def queue_gather(shard, after=None):
    folded = lax.all_gather(shard, "tok", axis=0, tiled=False, axis_index_groups=[list(FOLD)])
    if after is not None:
        folded, after = lax.optimization_barrier((folded, after))
    pairs = jnp.stack([folded[:4], jnp.flip(folded[4:], axis=0)], axis=1)
    return pairs.reshape(8 * shard.shape[0], shard.shape[1]), after


def fold_rows(full):
    pairs = full.reshape(4, 2, full.shape[0] // 8, full.shape[1])
    folded = jnp.concatenate([pairs[:, 0], jnp.flip(pairs[:, 1], axis=0)], axis=0)
    return folded.reshape(full.shape)


def queue_scatter(folded):
    return lax.psum_scatter(
        folded, "tok", scatter_dimension=0, tiled=True, axis_index_groups=[list(FOLD)]
    )


def core_gather(shard):
    upper = lax.axis_index("tok") >= 4
    other = lax.ppermute(shard, "tok", FAR_HALF)
    pair = jnp.stack([jnp.where(upper, other, shard), jnp.where(upper, shard, other)])
    every = spread(pair, "tok", 4, QUADS)
    return jnp.transpose(every, (1, 0, 2, 3)).reshape(8 * shard.shape[0], shard.shape[1])


def core_scatter(full):
    upper = lax.axis_index("tok") >= 4
    rows = full.shape[0] // 8
    blocks = jnp.transpose(full.reshape(2, 4, rows, full.shape[1]), (1, 0, 2, 3))
    pair = jnp.sum(lax.all_to_all(blocks, "tok", 0, 0, axis_index_groups=QUADS), axis=0)
    keep = jnp.where(upper, pair[1], pair[0])
    send = jnp.where(upper, pair[0], pair[1])
    return keep + lax.ppermute(send, "tok", FAR_HALF)


def on_device(
    tokens,
    targets,
    sample_ids,
    labels,
    utility,
    ref_loss,
    w_in,
    w_out,
    m_in,
    m_out,
    v_in,
    v_out,
    e_in,
    e_out,
):
    w_in_block = core_gather(w_in)
    id_lanes = jnp.broadcast_to(sample_ids.astype(jnp.float32)[:, None], (16, 128))
    rows_and_ids = spread(jnp.concatenate([tokens, id_lanes], axis=1), "hid", 8)
    rows_and_ids = rows_and_ids.reshape(128, 512)
    all_rows = rows_and_ids[:, :384]
    all_ids = rows_and_ids[:, 384].astype(jnp.int32)
    onehot = (all_ids[:, None] == jnp.arange(SAMPLES, dtype=jnp.int32)[None, :]).astype(
        jnp.float32
    )
    hidden = far_sum(y_sum(product(all_rows, w_in_block, 1, 0)))
    active_rows, slope_rows = gelu_parts(hidden)
    active = y_gather(active_rows)
    w_out_block, active = queue_gather(w_out, active)

    output = scatter_sum(product(active, w_out_block, 1, 0), "hid", 8)
    error = spread(output - targets, "hid", 8).reshape(128, 384)
    d_quarter = y_sum(product(error, w_out_block, 1, 1))
    d_active = far_sum(d_quarter)

    token_sq = jnp.sum(error * error, axis=1)
    local_sq = jnp.sum(token_sq[:, None] * onehot, axis=0)
    leading = lax.axis_index("inp") == 0
    local_counts = jnp.sum(onehot, axis=0) * jnp.where(leading, 1.0, 0.0)
    stats = jnp.concatenate([local_sq, local_counts, jnp.zeros((96,), jnp.float32)])[None, :]
    stats, d_quarter = lax.optimization_barrier((stats, d_quarter))
    stats = jnp.sum(spread(stats, ("inp", "tok"), 64), axis=(0, 1))
    loss, sample_coef = kto_terms(
        stats[:SAMPLES], stats[SAMPLES : 2 * SAMPLES], labels, utility, ref_loss
    )
    coef = jnp.sum(onehot * sample_coef[None, :], axis=1)[:, None]
    own_rows = lax.rem(lax.axis_index("inp"), 4) * 32
    own_coef = lax.dynamic_slice(coef, (own_rows, 0), (32, 1))

    grad_fold = fold_rows(product(active, error * coef, 0, 0))
    d_rows = d_active * own_coef * slope_rows
    grad_fold, d_rows = lax.optimization_barrier((grad_fold, d_rows))
    grad_out = queue_scatter(grad_fold)
    d_hidden = y_gather(d_rows)
    grad_in = core_scatter(product(all_rows, d_hidden, 0, 0))

    weight_out, new_m_out, new_v_out, new_e_out = adamw(w_out, m_out, v_out, e_out, grad_out)
    new_w_out, _ = queue_gather(weight_out)
    weight_in, new_m_in, new_v_in, new_e_in = adamw(w_in, m_in, v_in, e_in, grad_in)
    new_w_in = core_gather(weight_in)
    return (
        loss,
        new_w_in,
        new_w_out,
        new_m_in,
        new_m_out,
        new_v_in,
        new_v_out,
        new_e_in,
        new_e_out,
    )


def solution(mesh):
    in_specs = (
        P(("tok", "hid"), "inp"),
        P(("tok", "hid"), "inp"),
        P(("tok", "hid")),
        P(),
        P(),
        P(),
        P(("inp", "tok"), "hid"),
        P(("hid", "tok"), "inp"),
        P(("inp", "tok"), "hid"),
        P(("hid", "tok"), "inp"),
        P(("inp", "tok"), "hid"),
        P(("hid", "tok"), "inp"),
        P(("inp", "tok"), "hid"),
        P(("hid", "tok"), "inp"),
    )
    out_specs = (
        P(),
        P("inp", "hid"),
        P("hid", "inp"),
        P(("inp", "tok"), "hid"),
        P(("hid", "tok"), "inp"),
        P(("inp", "tok"), "hid"),
        P(("hid", "tok"), "inp"),
        P(("inp", "tok"), "hid"),
        P(("hid", "tok"), "inp"),
    )
    return jax.shard_map(
        on_device, mesh=mesh, in_specs=in_specs, out_specs=out_specs, check_vma=False
    )
```

```python
import jax
import jax.numpy as jnp
from jax import lax
from jax.sharding import PartitionSpec as P

D = 3072
SAMPLES = 16


mixed = lax.Precision.HIGH
highest = lax.Precision.HIGHEST
gelu_c = 0.7978845608028654
gelu_k = 0.044715
kto_beta = 4.0
loss_scale = 1048576.0
beta_one = 0.9
beta_two = 0.95
adam_eps = 1e-08
learn_rate = 0.001
decay_rate = 0.1
ema_rate = 0.99
bias_one = 1.0 - 0.9**10
bias_two = 1.0 - 0.95**10


QUADS = [[0, 1, 2, 3], [4, 5, 6, 7]]
FAR_HALF = [(i, (i + 4) % 8) for i in range(8)]
FOLD = (0, 2, 4, 6, 7, 5, 3, 1)


def gelu_parts(hidden):
    inner = gelu_c * (hidden + gelu_k * hidden * hidden * hidden)
    tangent = jnp.tanh(inner)
    active = 0.5 * hidden * (1.0 + tangent)
    slope = 0.5 * (1.0 + tangent) + 0.5 * hidden * (1.0 - tangent * tangent) * gelu_c * (
        1.0 + 3.0 * gelu_k * hidden * hidden
    )
    return (active, slope)


def adamw(weight, moment_one, moment_two, average, gradient):
    moment_one = beta_one * moment_one + (1.0 - beta_one) * gradient
    moment_two = beta_two * moment_two + (1.0 - beta_two) * gradient * gradient
    update = learn_rate * (moment_one / bias_one) / (jnp.sqrt(moment_two / bias_two) + adam_eps)
    weight = weight - update - learn_rate * decay_rate * weight
    average = ema_rate * average + (1.0 - ema_rate) * weight
    return (weight, moment_one, moment_two, average)


def kto_terms(sq_sums, counts, labels, utility, ref_loss):
    sample_loss = sq_sums / (counts * D)
    signs = 2.0 * labels.astype(jnp.float32) - 1.0
    chosen = jax.nn.sigmoid(signs * kto_beta * (ref_loss - sample_loss))
    loss = -jnp.sum(utility * chosen) / SAMPLES
    dloss = utility * chosen * (1.0 - chosen) * signs * kto_beta / SAMPLES
    sample_coef = loss_scale * 2.0 * dloss / (counts * D)
    return (loss, sample_coef)


def product(left, right, left_dim, right_dim):
    return lax.dot_general(
        left,
        right,
        (((left_dim,), (right_dim,)), ((), ())),
        precision=mixed,
        preferred_element_type=jnp.float32,
    )


def scatter_sum(part, axis, size, groups=None):
    blocks = part.reshape(size, part.shape[0] // size, part.shape[1])
    return jnp.sum(lax.all_to_all(blocks, axis, 0, 0, axis_index_groups=groups), axis=0)


def spread(block, axis, size, groups=None):
    copies = jnp.broadcast_to(block[None], (size,) + block.shape)
    return lax.all_to_all(copies, axis, 0, 0, axis_index_groups=groups)


def y_sum(part):
    return scatter_sum(part, "inp", 4, QUADS)


def far_sum(quarter):
    return quarter + lax.ppermute(quarter, "inp", FAR_HALF)


def y_gather(block):
    every = spread(block, "inp", 4, QUADS)
    return every.reshape(4 * block.shape[0], block.shape[1])


def queue_gather(shard, after=None):
    folded = lax.all_gather(shard, "tok", axis=0, tiled=False, axis_index_groups=[list(FOLD)])
    if after is not None:
        folded, after = lax.optimization_barrier((folded, after))
    return ring_order(folded).reshape(8 * shard.shape[0], shard.shape[1]), after


def fold_rows(full):
    pairs = full.reshape(4, 2, full.shape[0] // 8, full.shape[1])
    folded = jnp.concatenate([pairs[:, 0], jnp.flip(pairs[:, 1], axis=0)], axis=0)
    return folded.reshape(full.shape)


def queue_scatter(folded):
    return lax.psum_scatter(
        folded, "tok", scatter_dimension=0, tiled=True, axis_index_groups=[list(FOLD)]
    )


def ring_order(folded):
    pairs = jnp.stack([folded[:4], jnp.flip(folded[4:], axis=0)], axis=1)
    return pairs.reshape((8,) + folded.shape[1:])


def core_gather(shard, split):
    small = spread(shard[split:], "tok", 8)
    large = lax.all_gather(
        shard[:split], "tok", axis=0, tiled=False, axis_index_groups=[list(FOLD)]
    )
    every = jnp.concatenate([ring_order(large), small], axis=1)
    return every.reshape(8 * shard.shape[0], shard.shape[1])


def core_scatter(full, partner):
    upper = lax.axis_index("tok") >= 4
    rows = full.shape[0] // 8
    blocks = jnp.transpose(full.reshape(2, 4, rows, full.shape[1]), (1, 0, 2, 3))
    pair = jnp.sum(lax.all_to_all(blocks, "tok", 0, 0, axis_index_groups=QUADS), axis=0)
    pair, partner = lax.optimization_barrier((pair, partner))
    keep = jnp.where(upper, pair[1], pair[0])
    send = jnp.where(upper, pair[0], pair[1])
    return keep + lax.ppermute(send, "tok", FAR_HALF), partner


def on_device(
    tokens,
    targets,
    sample_ids,
    labels,
    utility,
    ref_loss,
    w_in,
    w_out,
    m_in,
    m_out,
    v_in,
    v_out,
    e_in,
    e_out,
):
    w_in_block = core_gather(w_in, 40)
    id_lanes = jnp.broadcast_to(sample_ids.astype(jnp.float32)[:, None], (16, 128))
    rows_and_ids = spread(jnp.concatenate([tokens, id_lanes], axis=1), "hid", 8)
    rows_and_ids = rows_and_ids.reshape(128, 512)
    all_rows = rows_and_ids[:, :384]
    all_ids = rows_and_ids[:, 384].astype(jnp.int32)
    onehot = (all_ids[:, None] == jnp.arange(SAMPLES, dtype=jnp.int32)[None, :]).astype(
        jnp.float32
    )
    hidden = far_sum(y_sum(product(all_rows, w_in_block, 1, 0)))
    active_rows, slope_rows = gelu_parts(hidden)
    active = y_gather(active_rows)
    w_out_block, active = queue_gather(w_out, active)

    output = scatter_sum(product(active, w_out_block, 1, 0), "hid", 8)
    error = spread(output - targets, "hid", 8).reshape(128, 384)
    token_sq = jnp.sum(error * error, axis=1)
    local_sq = jnp.sum(token_sq[:, None] * onehot, axis=0)
    leading = lax.axis_index("inp") == 0
    local_counts = jnp.sum(onehot, axis=0) * jnp.where(leading, 1.0, 0.0)
    stats = jnp.concatenate([local_sq, local_counts, jnp.zeros((96,), jnp.float32)])[None, :]
    d_quarter = y_sum(product(error, w_out_block, 1, 1))
    stats, d_quarter = lax.optimization_barrier((stats, d_quarter))
    stats = jnp.sum(spread(stats, ("inp", "tok"), 64), axis=(0, 1))
    d_active = far_sum(d_quarter)
    loss, sample_coef = kto_terms(
        stats[:SAMPLES], stats[SAMPLES : 2 * SAMPLES], labels, utility, ref_loss
    )
    coef = jnp.sum(onehot * sample_coef[None, :], axis=1)[:, None]
    own_rows = lax.rem(lax.axis_index("inp"), 4) * 32
    own_coef = lax.dynamic_slice(coef, (own_rows, 0), (32, 1))

    grad_fold = fold_rows(product(active, error * coef, 0, 0))
    d_rows = d_active * own_coef * slope_rows
    grad_fold, d_rows = lax.optimization_barrier((grad_fold, d_rows))
    grad_out = queue_scatter(grad_fold)
    d_hidden = y_gather(d_rows)
    grad_in, grad_out = core_scatter(product(all_rows, d_hidden, 0, 0), grad_out)

    weight_out, new_m_out, new_v_out, new_e_out = adamw(w_out, m_out, v_out, e_out, grad_out)
    new_w_out, _ = queue_gather(weight_out)
    weight_in, new_m_in, new_v_in, new_e_in = adamw(w_in, m_in, v_in, e_in, grad_in)
    new_w_in = core_gather(weight_in, 40)
    return (
        loss,
        new_w_in,
        new_w_out,
        new_m_in,
        new_m_out,
        new_v_in,
        new_v_out,
        new_e_in,
        new_e_out,
    )


def solution(mesh):
    in_specs = (
        P(("tok", "hid"), "inp"),
        P(("tok", "hid"), "inp"),
        P(("tok", "hid")),
        P(),
        P(),
        P(),
        P(("inp", "tok"), "hid"),
        P(("hid", "tok"), "inp"),
        P(("inp", "tok"), "hid"),
        P(("hid", "tok"), "inp"),
        P(("inp", "tok"), "hid"),
        P(("hid", "tok"), "inp"),
        P(("inp", "tok"), "hid"),
        P(("hid", "tok"), "inp"),
    )
    out_specs = (
        P(),
        P("inp", "hid"),
        P("hid", "inp"),
        P(("inp", "tok"), "hid"),
        P(("hid", "tok"), "inp"),
        P(("inp", "tok"), "hid"),
        P(("hid", "tok"), "inp"),
        P(("inp", "tok"), "hid"),
        P(("hid", "tok"), "inp"),
    )
    return jax.shard_map(
        on_device, mesh=mesh, in_specs=in_specs, out_specs=out_specs, check_vma=False
    )
```

```python
import jax
import jax.numpy as jnp
from jax import lax
from jax.sharding import PartitionSpec as P


D = 3072
SAMPLES = 16


mixed = lax.Precision.HIGH
gelu_c = 0.7978845608028654
gelu_k = 0.044715
kto_beta = 4.0
loss_scale = 1048576.0
beta_one = 0.9
beta_two = 0.95
adam_eps = 1e-08
learn_rate = 0.001
decay_rate = 0.1
ema_rate = 0.99
bias_one = 1.0 - 0.9**10
bias_two = 1.0 - 0.95**10


QUADS = [[0, 1, 2, 3], [4, 5, 6, 7]]
FAR_HALF = [(i, (i + 4) % 8) for i in range(8)]
FOLD = (0, 2, 4, 6, 7, 5, 3, 1)


def gelu_parts(hidden):
    inner = gelu_c * (hidden + gelu_k * hidden * hidden * hidden)
    tangent = jnp.tanh(inner)
    active = 0.5 * hidden * (1.0 + tangent)
    slope = 0.5 * (1.0 + tangent) + 0.5 * hidden * (1.0 - tangent * tangent) * gelu_c * (
        1.0 + 3.0 * gelu_k * hidden * hidden
    )
    return (active, slope)


def adamw(weight, moment_one, moment_two, average, gradient):
    moment_one = beta_one * moment_one + (1.0 - beta_one) * gradient
    moment_two = beta_two * moment_two + (1.0 - beta_two) * gradient * gradient
    update = learn_rate * (moment_one / bias_one) / (jnp.sqrt(moment_two / bias_two) + adam_eps)
    weight = weight - update - learn_rate * decay_rate * weight
    average = ema_rate * average + (1.0 - ema_rate) * weight
    return (weight, moment_one, moment_two, average)


def kto_terms(sq_sums, counts, labels, utility, ref_loss):
    sample_loss = sq_sums / (counts * D)
    signs = 2.0 * labels.astype(jnp.float32) - 1.0
    chosen = jax.nn.sigmoid(signs * kto_beta * (ref_loss - sample_loss))
    loss = -jnp.sum(utility * chosen) / SAMPLES
    dloss = utility * chosen * (1.0 - chosen) * signs * kto_beta / SAMPLES
    sample_coef = loss_scale * 2.0 * dloss / (counts * D)
    return (loss, sample_coef)


def product(left, right, left_dim, right_dim):
    return lax.dot_general(
        left,
        right,
        (((left_dim,), (right_dim,)), ((), ())),
        precision=mixed,
        preferred_element_type=jnp.float32,
    )


def scatter_sum(part, axis, size, groups=None):
    blocks = part.reshape(size, part.shape[0] // size, part.shape[1])
    return jnp.sum(lax.all_to_all(blocks, axis, 0, 0, axis_index_groups=groups), axis=0)


def spread(block, axis, size, groups=None):
    copies = jnp.broadcast_to(block[None], (size,) + block.shape)
    return lax.all_to_all(copies, axis, 0, 0, axis_index_groups=groups)


def y_sum(part):
    return scatter_sum(part, "inp", 4, QUADS)


def far_sum(quarter):
    return quarter + lax.ppermute(quarter, "inp", FAR_HALF)


def y_gather(block):
    every = spread(block, "inp", 4, QUADS)
    return every.reshape(4 * block.shape[0], block.shape[1])


def queue_gather(shard, after=None):
    folded = lax.all_gather(shard, "tok", axis=0, tiled=False, axis_index_groups=[list(FOLD)])
    if after is not None:
        folded, after = lax.optimization_barrier((folded, after))
    return ring_order(folded).reshape(8 * shard.shape[0], shard.shape[1]), after


def fold_rows(full):
    pairs = full.reshape(4, 2, full.shape[0] // 8, full.shape[1])
    folded = jnp.concatenate([pairs[:, 0], jnp.flip(pairs[:, 1], axis=0)], axis=0)
    return folded.reshape(full.shape)


def queue_scatter(folded):
    return lax.psum_scatter(
        folded, "tok", scatter_dimension=0, tiled=True, axis_index_groups=[list(FOLD)]
    )


def ring_order(folded):
    pairs = jnp.stack([folded[:4], jnp.flip(folded[4:], axis=0)], axis=1)
    return pairs.reshape((8,) + folded.shape[1:])


def core_gather(shard, split):
    small = spread(shard[split:], "tok", 8)
    large = lax.all_gather(
        shard[:split], "tok", axis=0, tiled=False, axis_index_groups=[list(FOLD)]
    )
    every = jnp.concatenate([ring_order(large), small], axis=1)
    return every.reshape(8 * shard.shape[0], shard.shape[1])


def core_scatter(full, partner):
    upper = lax.axis_index("tok") >= 4
    rows = full.shape[0] // 8
    blocks = jnp.transpose(full.reshape(2, 4, rows, full.shape[1]), (1, 0, 2, 3))
    pair = jnp.sum(lax.all_to_all(blocks, "tok", 0, 0, axis_index_groups=QUADS), axis=0)
    keep = jnp.where(upper, pair[1], pair[0])
    send = jnp.where(upper, pair[0], pair[1])
    keep, partner = lax.optimization_barrier((keep, partner))
    other = lax.ppermute(send, "tok", FAR_HALF)
    return keep + other, partner


def on_device(
    tokens,
    targets,
    sample_ids,
    labels,
    utility,
    ref_loss,
    w_in,
    w_out,
    m_in,
    m_out,
    v_in,
    v_out,
    e_in,
    e_out,
):
    w_in_block = core_gather(w_in, 40)
    id_lanes = jnp.broadcast_to(sample_ids.astype(jnp.float32)[:, None], (16, 128))
    rows_and_ids = spread(jnp.concatenate([tokens, id_lanes], axis=1), "hid", 8)
    rows_and_ids = rows_and_ids.reshape(128, 512)
    all_rows = rows_and_ids[:, :384]
    all_ids = rows_and_ids[:, 384].astype(jnp.int32)
    onehot = (all_ids[:, None] == jnp.arange(SAMPLES, dtype=jnp.int32)[None, :]).astype(
        jnp.float32
    )
    hidden = far_sum(y_sum(product(all_rows, w_in_block, 1, 0)))
    active_rows, slope_rows = gelu_parts(hidden)
    active = y_gather(active_rows)
    w_out_block, active = queue_gather(w_out, active)

    output = scatter_sum(product(active, w_out_block, 1, 0), "hid", 8)
    error = spread(output - targets, "hid", 8).reshape(128, 384)
    token_sq = jnp.sum(error * error, axis=1)
    local_sq = jnp.sum(token_sq[:, None] * onehot, axis=0)
    leading = lax.axis_index("inp") == 0
    local_counts = jnp.sum(onehot, axis=0) * jnp.where(leading, 1.0, 0.0)
    stats = jnp.concatenate([local_sq, local_counts, jnp.zeros((96,), jnp.float32)])[None, :]
    d_quarter = y_sum(product(error, w_out_block, 1, 1))
    stats, d_quarter = lax.optimization_barrier((stats, d_quarter))
    stats = jnp.sum(spread(stats, ("inp", "tok"), 64), axis=(0, 1))
    d_active = far_sum(d_quarter)
    loss, sample_coef = kto_terms(
        stats[:SAMPLES], stats[SAMPLES : 2 * SAMPLES], labels, utility, ref_loss
    )
    coef = jnp.sum(onehot * sample_coef[None, :], axis=1)[:, None]
    own_rows = lax.rem(lax.axis_index("inp"), 4) * 32
    own_coef = lax.dynamic_slice(coef, (own_rows, 0), (32, 1))

    grad_fold = fold_rows(product(active, error * coef, 0, 0))
    d_rows = d_active * own_coef * slope_rows
    grad_fold, d_rows = lax.optimization_barrier((grad_fold, d_rows))
    grad_out = queue_scatter(grad_fold)
    d_hidden = y_gather(d_rows)
    grad_in, grad_out = core_scatter(product(all_rows, d_hidden, 0, 0), grad_out)

    weight_out, new_m_out, new_v_out, new_e_out = adamw(w_out, m_out, v_out, e_out, grad_out)
    new_w_out, _ = queue_gather(weight_out)
    weight_in, new_m_in, new_v_in, new_e_in = adamw(w_in, m_in, v_in, e_in, grad_in)
    new_w_in = core_gather(weight_in, 40)
    return (
        loss,
        new_w_in,
        new_w_out,
        new_m_in,
        new_m_out,
        new_v_in,
        new_v_out,
        new_e_in,
        new_e_out,
    )


def solution(mesh):
    in_specs = (
        P(("tok", "hid"), "inp"),
        P(("tok", "hid"), "inp"),
        P(("tok", "hid")),
        P(),
        P(),
        P(),
        P(("inp", "tok"), "hid"),
        P(("hid", "tok"), "inp"),
        P(("inp", "tok"), "hid"),
        P(("hid", "tok"), "inp"),
        P(("inp", "tok"), "hid"),
        P(("hid", "tok"), "inp"),
        P(("inp", "tok"), "hid"),
        P(("hid", "tok"), "inp"),
    )
    out_specs = (
        P(),
        P("inp", "hid"),
        P("hid", "inp"),
        P(("inp", "tok"), "hid"),
        P(("hid", "tok"), "inp"),
        P(("inp", "tok"), "hid"),
        P(("hid", "tok"), "inp"),
        P(("inp", "tok"), "hid"),
        P(("hid", "tok"), "inp"),
    )
    return jax.shard_map(
        on_device, mesh=mesh, in_specs=in_specs, out_specs=out_specs, check_vma=False
    )
```

```python
import jax
import jax.numpy as jnp
from jax import lax
from jax.sharding import PartitionSpec as P


D = 3072
SAMPLES = 16


mixed = lax.Precision.HIGH
gelu_c = 0.7978845608028654
gelu_k = 0.044715
kto_beta = 4.0
loss_scale = 1048576.0
beta_one = 0.9
beta_two = 0.95
adam_eps = 1e-08
learn_rate = 0.001
decay_rate = 0.1
ema_rate = 0.99
bias_one = 1.0 - 0.9**10
bias_two = 1.0 - 0.95**10


QUADS = [[0, 1, 2, 3], [4, 5, 6, 7]]
FAR_HALF = [(i, (i + 4) % 8) for i in range(8)]
FOLD = (0, 2, 4, 6, 7, 5, 3, 1)


def gelu_parts(hidden):
    inner = gelu_c * (hidden + gelu_k * hidden * hidden * hidden)
    tangent = jnp.tanh(inner)
    active = 0.5 * hidden * (1.0 + tangent)
    slope = 0.5 * (1.0 + tangent) + 0.5 * hidden * (1.0 - tangent * tangent) * gelu_c * (
        1.0 + 3.0 * gelu_k * hidden * hidden
    )
    return (active, slope)


def adamw(weight, moment_one, moment_two, average, gradient):
    moment_one = beta_one * moment_one + (1.0 - beta_one) * gradient
    moment_two = beta_two * moment_two + (1.0 - beta_two) * gradient * gradient
    update = learn_rate * (moment_one / bias_one) / (jnp.sqrt(moment_two / bias_two) + adam_eps)
    weight = weight - update - learn_rate * decay_rate * weight
    average = ema_rate * average + (1.0 - ema_rate) * weight
    return (weight, moment_one, moment_two, average)


def kto_terms(sq_sums, counts, labels, utility, ref_loss):
    sample_loss = sq_sums / (counts * D)
    signs = 2.0 * labels.astype(jnp.float32) - 1.0
    chosen = jax.nn.sigmoid(signs * kto_beta * (ref_loss - sample_loss))
    loss = -jnp.sum(utility * chosen) / SAMPLES
    dloss = utility * chosen * (1.0 - chosen) * signs * kto_beta / SAMPLES
    sample_coef = loss_scale * 2.0 * dloss / (counts * D)
    return (loss, sample_coef)


def product(left, right, left_dim, right_dim):
    return lax.dot_general(
        left,
        right,
        (((left_dim,), (right_dim,)), ((), ())),
        precision=mixed,
        preferred_element_type=jnp.float32,
    )


def scatter_sum(part, axis, size, groups=None):
    blocks = part.reshape(size, part.shape[0] // size, part.shape[1])
    return jnp.sum(lax.all_to_all(blocks, axis, 0, 0, axis_index_groups=groups), axis=0)


def spread(block, axis, size, groups=None):
    copies = jnp.broadcast_to(block[None], (size,) + block.shape)
    return lax.all_to_all(copies, axis, 0, 0, axis_index_groups=groups)


def y_sum(part):
    return scatter_sum(part, "inp", 4, QUADS)


def far_sum(quarter):
    return quarter + lax.ppermute(quarter, "inp", FAR_HALF)


def y_gather(block):
    every = spread(block, "inp", 4, QUADS)
    return every.reshape(4 * block.shape[0], block.shape[1])


def queue_gather(shard, after=None):
    folded = lax.all_gather(shard, "tok", axis=0, tiled=False, axis_index_groups=[list(FOLD)])
    if after is not None:
        folded, after = lax.optimization_barrier((folded, after))
    return ring_order(folded).reshape(8 * shard.shape[0], shard.shape[1]), after


def fold_rows(full):
    pairs = full.reshape(4, 2, full.shape[0] // 8, full.shape[1])
    folded = jnp.concatenate([pairs[:, 0], jnp.flip(pairs[:, 1], axis=0)], axis=0)
    return folded.reshape(full.shape)


def queue_scatter(folded):
    return lax.psum_scatter(
        folded, "tok", scatter_dimension=0, tiled=True, axis_index_groups=[list(FOLD)]
    )


def ring_order(folded):
    pairs = jnp.stack([folded[:4], jnp.flip(folded[4:], axis=0)], axis=1)
    return pairs.reshape((8,) + folded.shape[1:])


def core_gather(shard, split):
    small = spread(shard[split:], "tok", 8)
    large = lax.all_gather(
        shard[:split], "tok", axis=0, tiled=False, axis_index_groups=[list(FOLD)]
    )
    every = jnp.concatenate([ring_order(large), small], axis=1)
    return every.reshape(8 * shard.shape[0], shard.shape[1])


def quad_columns(rows):
    blocks = jnp.transpose(rows.reshape(128, 2, 4, 48), (2, 0, 1, 3)).reshape(4, 128, 96)
    every = lax.all_to_all(blocks, "tok", 0, 0, axis_index_groups=QUADS)
    return jnp.transpose(every.reshape(4, 4, 32, 96), (1, 0, 2, 3)).reshape(512, 96)


def quad_rows(block):
    near = spread(block, "tok", 4, QUADS).reshape(128, 768)
    return spread(near, "inp", 4, QUADS).reshape(512, 768)


def half_sum(pair, partner):
    upper = lax.axis_index("tok") >= 4
    rows = pair.shape[0] // 2
    keep = jnp.where(upper, pair[rows:], pair[:rows])
    send = jnp.where(upper, pair[:rows], pair[rows:])
    keep, partner = lax.optimization_barrier((keep, partner))
    other = lax.ppermute(send, "tok", FAR_HALF)
    return keep + other, partner


def on_device(
    tokens,
    targets,
    sample_ids,
    labels,
    utility,
    ref_loss,
    w_in,
    w_out,
    m_in,
    m_out,
    v_in,
    v_out,
    e_in,
    e_out,
):
    w_in_block, _ = queue_gather(w_in)
    id_lanes = jnp.broadcast_to(sample_ids.astype(jnp.float32)[:, None], (16, 128))
    rows_and_ids = spread(jnp.concatenate([tokens, id_lanes], axis=1), "hid", 8)
    rows_and_ids = rows_and_ids.reshape(128, 512)
    all_rows = rows_and_ids[:, :384]
    all_rows, columns = lax.optimization_barrier((all_rows, quad_columns(all_rows)))
    all_ids = rows_and_ids[:, 384].astype(jnp.int32)
    onehot = (all_ids[:, None] == jnp.arange(SAMPLES, dtype=jnp.int32)[None, :]).astype(
        jnp.float32
    )
    hidden = far_sum(y_sum(product(all_rows, w_in_block, 1, 0)))
    active_rows, slope_rows = gelu_parts(hidden)
    active = y_gather(active_rows)
    w_out_block, active = queue_gather(w_out, active)

    output = scatter_sum(product(active, w_out_block, 1, 0), "hid", 8)
    error = spread(output - targets, "hid", 8).reshape(128, 384)
    token_sq = jnp.sum(error * error, axis=1)
    local_sq = jnp.sum(token_sq[:, None] * onehot, axis=0)
    leading = lax.axis_index("inp") == 0
    local_counts = jnp.sum(onehot, axis=0) * jnp.where(leading, 1.0, 0.0)
    stats = jnp.concatenate([local_sq, local_counts, jnp.zeros((96,), jnp.float32)])[None, :]
    d_quarter = y_sum(product(error, w_out_block, 1, 1))
    stats, d_quarter = lax.optimization_barrier((stats, d_quarter))
    stats = jnp.sum(spread(stats, ("inp", "tok"), 64), axis=(0, 1))
    d_active = far_sum(d_quarter)
    loss, sample_coef = kto_terms(
        stats[:SAMPLES], stats[SAMPLES : 2 * SAMPLES], labels, utility, ref_loss
    )
    coef = jnp.sum(onehot * sample_coef[None, :], axis=1)[:, None]
    own_rows = lax.rem(lax.axis_index("inp"), 4) * 32
    own_coef = lax.dynamic_slice(coef, (own_rows, 0), (32, 1))

    grad_fold = fold_rows(product(active, error * coef, 0, 0))
    d_rows = d_active * own_coef * slope_rows
    grad_fold, d_rows = lax.optimization_barrier((grad_fold, d_rows))
    grad_out = queue_scatter(grad_fold)
    grad_in, grad_out = half_sum(product(columns, quad_rows(d_rows), 0, 0), grad_out)

    weight_out, new_m_out, new_v_out, new_e_out = adamw(w_out, m_out, v_out, e_out, grad_out)
    new_w_out, _ = queue_gather(weight_out)
    weight_in, new_m_in, new_v_in, new_e_in = adamw(w_in, m_in, v_in, e_in, grad_in)
    new_w_in = core_gather(weight_in, 40)
    return (
        loss,
        new_w_in,
        new_w_out,
        new_m_in,
        new_m_out,
        new_v_in,
        new_v_out,
        new_e_in,
        new_e_out,
    )


def solution(mesh):
    in_specs = (
        P(("tok", "hid"), "inp"),
        P(("tok", "hid"), "inp"),
        P(("tok", "hid")),
        P(),
        P(),
        P(),
        P(("inp", "tok"), "hid"),
        P(("hid", "tok"), "inp"),
        P(("inp", "tok"), "hid"),
        P(("hid", "tok"), "inp"),
        P(("inp", "tok"), "hid"),
        P(("hid", "tok"), "inp"),
        P(("inp", "tok"), "hid"),
        P(("hid", "tok"), "inp"),
    )
    out_specs = (
        P(),
        P("inp", "hid"),
        P("hid", "inp"),
        P(("inp", "tok"), "hid"),
        P(("hid", "tok"), "inp"),
        P(("inp", "tok"), "hid"),
        P(("hid", "tok"), "inp"),
        P(("inp", "tok"), "hid"),
        P(("hid", "tok"), "inp"),
    )
    return jax.shard_map(
        on_device, mesh=mesh, in_specs=in_specs, out_specs=out_specs, check_vma=False
    )
```

```python
import jax
import jax.numpy as jnp
from jax import lax
from jax.sharding import PartitionSpec as P


D = 3072
SAMPLES = 16


mixed = lax.Precision.HIGH
gelu_c = 0.7978845608028654
gelu_k = 0.044715
kto_beta = 4.0
loss_scale = 1048576.0
beta_one = 0.9
beta_two = 0.95
adam_eps = 1e-08
learn_rate = 0.001
decay_rate = 0.1
ema_rate = 0.99
bias_one = 1.0 - 0.9**10
bias_two = 1.0 - 0.95**10


QUADS = [[0, 1, 2, 3], [4, 5, 6, 7]]
FAR_HALF = [(i, (i + 4) % 8) for i in range(8)]
FOLD = (0, 2, 4, 6, 7, 5, 3, 1)


def gelu_parts(hidden):
    inner = gelu_c * (hidden + gelu_k * hidden * hidden * hidden)
    tangent = jnp.tanh(inner)
    active = 0.5 * hidden * (1.0 + tangent)
    slope = 0.5 * (1.0 + tangent) + 0.5 * hidden * (1.0 - tangent * tangent) * gelu_c * (
        1.0 + 3.0 * gelu_k * hidden * hidden
    )
    return (active, slope)


def adamw(weight, moment_one, moment_two, average, gradient):
    moment_one = beta_one * moment_one + (1.0 - beta_one) * gradient
    moment_two = beta_two * moment_two + (1.0 - beta_two) * gradient * gradient
    update = learn_rate * (moment_one / bias_one) / (jnp.sqrt(moment_two / bias_two) + adam_eps)
    weight = weight - update - learn_rate * decay_rate * weight
    average = ema_rate * average + (1.0 - ema_rate) * weight
    return (weight, moment_one, moment_two, average)


def kto_terms(sq_sums, counts, labels, utility, ref_loss):
    sample_loss = sq_sums / (counts * D)
    signs = 2.0 * labels.astype(jnp.float32) - 1.0
    chosen = jax.nn.sigmoid(signs * kto_beta * (ref_loss - sample_loss))
    loss = -jnp.sum(utility * chosen) / SAMPLES
    dloss = utility * chosen * (1.0 - chosen) * signs * kto_beta / SAMPLES
    sample_coef = loss_scale * 2.0 * dloss / (counts * D)
    return (loss, sample_coef)


def product(left, right, left_dim, right_dim):
    return lax.dot_general(
        left,
        right,
        (((left_dim,), (right_dim,)), ((), ())),
        precision=mixed,
        preferred_element_type=jnp.float32,
    )


def scatter_sum(part, axis, size, groups=None):
    blocks = part.reshape(size, part.shape[0] // size, part.shape[1])
    return jnp.sum(lax.all_to_all(blocks, axis, 0, 0, axis_index_groups=groups), axis=0)


def spread(block, axis, size, groups=None):
    copies = jnp.broadcast_to(block[None], (size,) + block.shape)
    return lax.all_to_all(copies, axis, 0, 0, axis_index_groups=groups)


def y_sum(part):
    return scatter_sum(part, "inp", 4, QUADS)


def far_sum(quarter):
    return quarter + lax.ppermute(quarter, "inp", FAR_HALF)


def y_gather(block):
    every = spread(block, "inp", 4, QUADS)
    return every.reshape(4 * block.shape[0], block.shape[1])


def queue_gather(shard, after=None):
    folded = lax.all_gather(shard, "tok", axis=0, tiled=False, axis_index_groups=[list(FOLD)])
    if after is not None:
        folded, after = lax.optimization_barrier((folded, after))
    return ring_order(folded).reshape(8 * shard.shape[0], shard.shape[1]), after


def fold_rows(full):
    pairs = full.reshape(4, 2, full.shape[0] // 8, full.shape[1])
    folded = jnp.concatenate([pairs[:, 0], jnp.flip(pairs[:, 1], axis=0)], axis=0)
    return folded.reshape(full.shape)


def queue_scatter(folded):
    return lax.psum_scatter(
        folded, "tok", scatter_dimension=0, tiled=True, axis_index_groups=[list(FOLD)]
    )


def ring_order(folded):
    pairs = jnp.stack([folded[:4], jnp.flip(folded[4:], axis=0)], axis=1)
    return pairs.reshape((8,) + folded.shape[1:])


def core_gather(shard, split):
    small = spread(shard[split:], "tok", 8)
    large = lax.all_gather(
        shard[:split], "tok", axis=0, tiled=False, axis_index_groups=[list(FOLD)]
    )
    every = jnp.concatenate([ring_order(large), small], axis=1)
    return every.reshape(8 * shard.shape[0], shard.shape[1])


def half_pair(shard):
    upper = lax.axis_index("tok") >= 4
    other = lax.ppermute(shard, "tok", FAR_HALF)
    return jnp.concatenate([jnp.where(upper, other, shard), jnp.where(upper, shard, other)])


def quad_columns(tokens, sample_ids):
    blocks = jnp.transpose(tokens.reshape(16, 2, 4, 48), (2, 0, 1, 3)).reshape(4, 16, 96)
    id_lanes = jnp.broadcast_to(sample_ids.astype(jnp.float32)[None, :, None], (4, 16, 32))
    blocks = jnp.concatenate([blocks, id_lanes], axis=2)
    near = lax.all_to_all(blocks, "tok", 0, 0, axis_index_groups=QUADS)
    every = spread(near, "hid", 8).reshape(4, 2, 4, 16, 128)
    return jnp.transpose(every, (0, 2, 1, 3, 4)).reshape(512, 128)


def quad_rows(block):
    near = spread(block, "tok", 4, QUADS).reshape(128, 768)
    return spread(near, "inp", 4, QUADS).reshape(512, 768)


def half_sum(pair, partner):
    upper = lax.axis_index("tok") >= 4
    rows = pair.shape[0] // 2
    keep = jnp.where(upper, pair[rows:], pair[:rows])
    send = jnp.where(upper, pair[:rows], pair[rows:])
    keep, partner = lax.optimization_barrier((keep, partner))
    other = lax.ppermute(send, "tok", FAR_HALF)
    return keep + other, partner


def on_device(
    tokens,
    targets,
    sample_ids,
    labels,
    utility,
    ref_loss,
    w_in,
    w_out,
    m_in,
    m_out,
    v_in,
    v_out,
    e_in,
    e_out,
):
    w_in_pair = half_pair(w_in)
    table = quad_columns(tokens, sample_ids)
    columns = table[:, :96]
    quad_ids = table[:, 96].reshape(4, 4, 32)
    own_quad = lax.rem(lax.axis_index("tok"), 4)
    all_ids = lax.dynamic_index_in_dim(quad_ids, own_quad, axis=1, keepdims=False)
    all_ids = all_ids.reshape(-1).astype(jnp.int32)
    onehot = (all_ids[:, None] == jnp.arange(SAMPLES, dtype=jnp.int32)[None, :]).astype(
        jnp.float32
    )
    quad_part = y_sum(product(columns, w_in_pair, 1, 0))
    hidden = far_sum(scatter_sum(quad_part, "tok", 4, QUADS))
    active_rows, slope_rows = gelu_parts(hidden)
    active = y_gather(active_rows)
    w_out_block, active = queue_gather(w_out, active)

    output = scatter_sum(product(active, w_out_block, 1, 0), "hid", 8)
    error = spread(output - targets, "hid", 8).reshape(128, 384)
    token_sq = jnp.sum(error * error, axis=1)
    local_sq = jnp.sum(token_sq[:, None] * onehot, axis=0)
    leading = lax.axis_index("inp") == 0
    local_counts = jnp.sum(onehot, axis=0) * jnp.where(leading, 1.0, 0.0)
    stats = jnp.concatenate([local_sq, local_counts, jnp.zeros((96,), jnp.float32)])[None, :]
    d_quarter = y_sum(product(error, w_out_block, 1, 1))
    stats, d_quarter = lax.optimization_barrier((stats, d_quarter))
    stats = jnp.sum(spread(stats, ("inp", "tok"), 64), axis=(0, 1))
    d_active = far_sum(d_quarter)
    loss, sample_coef = kto_terms(
        stats[:SAMPLES], stats[SAMPLES : 2 * SAMPLES], labels, utility, ref_loss
    )
    coef = jnp.sum(onehot * sample_coef[None, :], axis=1)[:, None]
    own_rows = lax.rem(lax.axis_index("inp"), 4) * 32
    own_coef = lax.dynamic_slice(coef, (own_rows, 0), (32, 1))

    grad_fold = fold_rows(product(active, error * coef, 0, 0))
    d_rows = d_active * own_coef * slope_rows
    grad_fold, d_rows = lax.optimization_barrier((grad_fold, d_rows))
    grad_out = queue_scatter(grad_fold)
    grad_in, grad_out = half_sum(product(columns, quad_rows(d_rows), 0, 0), grad_out)

    weight_out, new_m_out, new_v_out, new_e_out = adamw(w_out, m_out, v_out, e_out, grad_out)
    new_w_out, _ = queue_gather(weight_out)
    weight_in, new_m_in, new_v_in, new_e_in = adamw(w_in, m_in, v_in, e_in, grad_in)
    new_w_in = core_gather(weight_in, 40)
    return (
        loss,
        new_w_in,
        new_w_out,
        new_m_in,
        new_m_out,
        new_v_in,
        new_v_out,
        new_e_in,
        new_e_out,
    )


def solution(mesh):
    in_specs = (
        P(("tok", "hid"), "inp"),
        P(("tok", "hid"), "inp"),
        P(("tok", "hid")),
        P(),
        P(),
        P(),
        P(("inp", "tok"), "hid"),
        P(("hid", "tok"), "inp"),
        P(("inp", "tok"), "hid"),
        P(("hid", "tok"), "inp"),
        P(("inp", "tok"), "hid"),
        P(("hid", "tok"), "inp"),
        P(("inp", "tok"), "hid"),
        P(("hid", "tok"), "inp"),
    )
    out_specs = (
        P(),
        P("inp", "hid"),
        P("hid", "inp"),
        P(("inp", "tok"), "hid"),
        P(("hid", "tok"), "inp"),
        P(("inp", "tok"), "hid"),
        P(("hid", "tok"), "inp"),
        P(("inp", "tok"), "hid"),
        P(("hid", "tok"), "inp"),
    )
    return jax.shard_map(
        on_device, mesh=mesh, in_specs=in_specs, out_specs=out_specs, check_vma=False
    )
```

```python
import jax
import jax.numpy as jnp
from jax import lax
from jax.sharding import PartitionSpec as P


D = 3072
SAMPLES = 16


mixed = lax.Precision.HIGH
gelu_c = 0.7978845608028654
gelu_k = 0.044715
kto_beta = 4.0
loss_scale = 1048576.0
beta_one = 0.9
beta_two = 0.95
adam_eps = 1e-08
learn_rate = 0.001
decay_rate = 0.1
ema_rate = 0.99
bias_one = 1.0 - 0.9**10
bias_two = 1.0 - 0.95**10


QUADS = [[0, 1, 2, 3], [4, 5, 6, 7]]
FAR_HALF = [(i, (i + 4) % 8) for i in range(8)]
FOLD = (0, 2, 4, 6, 7, 5, 3, 1)


def gelu_parts(hidden):
    inner = gelu_c * (hidden + gelu_k * hidden * hidden * hidden)
    tangent = jnp.tanh(inner)
    active = 0.5 * hidden * (1.0 + tangent)
    slope = 0.5 * (1.0 + tangent) + 0.5 * hidden * (1.0 - tangent * tangent) * gelu_c * (
        1.0 + 3.0 * gelu_k * hidden * hidden
    )
    return (active, slope)


def adamw(weight, moment_one, moment_two, average, gradient):
    moment_one = beta_one * moment_one + (1.0 - beta_one) * gradient
    moment_two = beta_two * moment_two + (1.0 - beta_two) * gradient * gradient
    update = learn_rate * (moment_one / bias_one) / (jnp.sqrt(moment_two / bias_two) + adam_eps)
    weight = weight - update - learn_rate * decay_rate * weight
    average = ema_rate * average + (1.0 - ema_rate) * weight
    return (weight, moment_one, moment_two, average)


def kto_terms(sq_sums, counts, labels, utility, ref_loss):
    sample_loss = sq_sums / (counts * D)
    signs = 2.0 * labels.astype(jnp.float32) - 1.0
    chosen = jax.nn.sigmoid(signs * kto_beta * (ref_loss - sample_loss))
    loss = -jnp.sum(utility * chosen) / SAMPLES
    dloss = utility * chosen * (1.0 - chosen) * signs * kto_beta / SAMPLES
    sample_coef = loss_scale * 2.0 * dloss / (counts * D)
    return (loss, sample_coef)


def product(left, right, left_dim, right_dim):
    return lax.dot_general(
        left,
        right,
        (((left_dim,), (right_dim,)), ((), ())),
        precision=mixed,
        preferred_element_type=jnp.float32,
    )


def scatter_sum(part, axis, size, groups=None):
    blocks = part.reshape(size, part.shape[0] // size, part.shape[1])
    return jnp.sum(lax.all_to_all(blocks, axis, 0, 0, axis_index_groups=groups), axis=0)


def spread(block, axis, size, groups=None):
    copies = jnp.broadcast_to(block[None], (size,) + block.shape)
    return lax.all_to_all(copies, axis, 0, 0, axis_index_groups=groups)


def y_sum(part):
    return scatter_sum(part, "inp", 4, QUADS)


def far_sum(quarter):
    return quarter + lax.ppermute(quarter, "inp", FAR_HALF)


def y_gather(block):
    every = spread(block, "inp", 4, QUADS)
    return every.reshape(4 * block.shape[0], block.shape[1])


def queue_gather(shard, after=None):
    folded = lax.all_gather(shard, "tok", axis=0, tiled=False, axis_index_groups=[list(FOLD)])
    if after is not None:
        folded, after = lax.optimization_barrier((folded, after))
    return ring_order(folded).reshape(8 * shard.shape[0], shard.shape[1]), after


def fold_rows(full):
    pairs = full.reshape(4, 2, full.shape[0] // 8, full.shape[1])
    folded = jnp.concatenate([pairs[:, 0], jnp.flip(pairs[:, 1], axis=0)], axis=0)
    return folded.reshape(full.shape)


def queue_scatter(folded):
    return lax.psum_scatter(
        folded, "tok", scatter_dimension=0, tiled=True, axis_index_groups=[list(FOLD)]
    )


def ring_order(folded):
    pairs = jnp.stack([folded[:4], jnp.flip(folded[4:], axis=0)], axis=1)
    return pairs.reshape((8,) + folded.shape[1:])


def core_gather(shard, split):
    small = spread(shard[split:], "tok", 8)
    large = lax.all_gather(
        shard[:split], "tok", axis=0, tiled=False, axis_index_groups=[list(FOLD)]
    )
    every = jnp.concatenate([ring_order(large), small], axis=1)
    return every.reshape(8 * shard.shape[0], shard.shape[1])


def half_pair(shard):
    upper = lax.axis_index("tok") >= 4
    other = lax.ppermute(shard, "tok", FAR_HALF)
    return jnp.concatenate([jnp.where(upper, other, shard), jnp.where(upper, shard, other)])


def quad_columns(tokens, sample_ids):
    blocks = jnp.transpose(tokens.reshape(16, 2, 4, 48), (2, 0, 1, 3)).reshape(4, 16, 96)
    id_lanes = jnp.broadcast_to(sample_ids.astype(jnp.float32)[None, :, None], (4, 16, 32))
    blocks = jnp.concatenate([blocks, id_lanes], axis=2)
    near = lax.all_to_all(blocks, "tok", 0, 0, axis_index_groups=QUADS)
    every = spread(near, "hid", 8).reshape(4, 2, 4, 16, 128)
    return jnp.transpose(every, (0, 2, 1, 3, 4)).reshape(512, 128)


def quad_rows(block):
    near = spread(block, "tok", 4, QUADS).reshape(128, 768)
    return spread(near, "inp", 4, QUADS).reshape(512, 768)


def half_sum(pair):
    upper = lax.axis_index("tok") >= 4
    rows = pair.shape[0] // 2
    keep = jnp.where(upper, pair[rows:], pair[:rows])
    send = jnp.where(upper, pair[:rows], pair[rows:])
    return keep + lax.ppermute(send, "tok", FAR_HALF)


def on_device(
    tokens,
    targets,
    sample_ids,
    labels,
    utility,
    ref_loss,
    w_in,
    w_out,
    m_in,
    m_out,
    v_in,
    v_out,
    e_in,
    e_out,
):
    w_in_pair = half_pair(w_in)
    table = quad_columns(tokens, sample_ids)
    columns = table[:, :96]
    quad_ids = table[:, 96].reshape(4, 4, 32)
    own_quad = lax.rem(lax.axis_index("tok"), 4)
    all_ids = lax.dynamic_index_in_dim(quad_ids, own_quad, axis=1, keepdims=False)
    all_ids = all_ids.reshape(-1).astype(jnp.int32)
    onehot = (all_ids[:, None] == jnp.arange(SAMPLES, dtype=jnp.int32)[None, :]).astype(
        jnp.float32
    )
    quad_part = y_sum(product(columns, w_in_pair, 1, 0))
    hidden = far_sum(scatter_sum(quad_part, "tok", 4, QUADS))
    active_rows, slope_rows = gelu_parts(hidden)
    active = y_gather(active_rows)
    w_out_block, active = queue_gather(w_out, active)

    output = scatter_sum(product(active, w_out_block, 1, 0), "hid", 8)
    error = spread(output - targets, "hid", 8).reshape(128, 384)
    token_sq = jnp.sum(error * error, axis=1)
    local_sq = jnp.sum(token_sq[:, None] * onehot, axis=0)
    leading = lax.axis_index("inp") == 0
    local_counts = jnp.sum(onehot, axis=0) * jnp.where(leading, 1.0, 0.0)
    stats = jnp.concatenate([local_sq, local_counts, jnp.zeros((96,), jnp.float32)])[None, :]
    stats = jnp.sum(spread(stats, ("inp", "tok"), 64), axis=(0, 1))
    loss, sample_coef = kto_terms(
        stats[:SAMPLES], stats[SAMPLES : 2 * SAMPLES], labels, utility, ref_loss
    )
    coef = jnp.sum(onehot * sample_coef[None, :], axis=1)[:, None]
    own_rows = lax.rem(lax.axis_index("inp"), 4) * 32
    own_coef = lax.dynamic_slice(coef, (own_rows, 0), (32, 1))

    grad_fold = fold_rows(product(active, error * coef, 0, 0))
    grad_fold, error = lax.optimization_barrier((grad_fold, error))
    grad_out = queue_scatter(grad_fold)
    d_active = far_sum(y_sum(product(error, w_out_block, 1, 1)))
    d_hidden = quad_rows(d_active * own_coef * slope_rows)
    d_hidden, grad_out = lax.optimization_barrier((d_hidden, grad_out))
    grad_in = half_sum(product(columns, d_hidden, 0, 0))

    weight_out, new_m_out, new_v_out, new_e_out = adamw(w_out, m_out, v_out, e_out, grad_out)
    new_w_out, _ = queue_gather(weight_out)
    weight_in, new_m_in, new_v_in, new_e_in = adamw(w_in, m_in, v_in, e_in, grad_in)
    new_w_in = core_gather(weight_in, 40)
    return (
        loss,
        new_w_in,
        new_w_out,
        new_m_in,
        new_m_out,
        new_v_in,
        new_v_out,
        new_e_in,
        new_e_out,
    )


def solution(mesh):
    in_specs = (
        P(("tok", "hid"), "inp"),
        P(("tok", "hid"), "inp"),
        P(("tok", "hid")),
        P(),
        P(),
        P(),
        P(("inp", "tok"), "hid"),
        P(("hid", "tok"), "inp"),
        P(("inp", "tok"), "hid"),
        P(("hid", "tok"), "inp"),
        P(("inp", "tok"), "hid"),
        P(("hid", "tok"), "inp"),
        P(("inp", "tok"), "hid"),
        P(("hid", "tok"), "inp"),
    )
    out_specs = (
        P(),
        P("inp", "hid"),
        P("hid", "inp"),
        P(("inp", "tok"), "hid"),
        P(("hid", "tok"), "inp"),
        P(("inp", "tok"), "hid"),
        P(("hid", "tok"), "inp"),
        P(("inp", "tok"), "hid"),
        P(("hid", "tok"), "inp"),
    )
    return jax.shard_map(
        on_device, mesh=mesh, in_specs=in_specs, out_specs=out_specs, check_vma=False
    )
```

```python
import jax
import jax.numpy as jnp
from jax import lax
from jax.sharding import PartitionSpec as P


D = 3072
SAMPLES = 16


mixed = lax.Precision.HIGH
gelu_c = 0.7978845608028654
gelu_k = 0.044715
kto_beta = 4.0
loss_scale = 1048576.0
beta_one = 0.9
beta_two = 0.95
adam_eps = 1e-08
learn_rate = 0.001
decay_rate = 0.1
ema_rate = 0.99
bias_one = 1.0 - 0.9**10
bias_two = 1.0 - 0.95**10


QUADS = [[0, 1, 2, 3], [4, 5, 6, 7]]
HID_QUADS = [[h * 8 + half + q for h in range(8) for q in range(4)] for half in (0, 4)]
FAR_HALF = [(i, (i + 4) % 8) for i in range(8)]
FOLD = (0, 2, 4, 6, 7, 5, 3, 1)


def gelu_parts(hidden):
    inner = gelu_c * (hidden + gelu_k * hidden * hidden * hidden)
    tangent = jnp.tanh(inner)
    active = 0.5 * hidden * (1.0 + tangent)
    slope = 0.5 * (1.0 + tangent) + 0.5 * hidden * (1.0 - tangent * tangent) * gelu_c * (
        1.0 + 3.0 * gelu_k * hidden * hidden
    )
    return (active, slope)


def adamw(weight, moment_one, moment_two, average, gradient):
    moment_one = beta_one * moment_one + (1.0 - beta_one) * gradient
    moment_two = beta_two * moment_two + (1.0 - beta_two) * gradient * gradient
    update = learn_rate * (moment_one / bias_one) / (jnp.sqrt(moment_two / bias_two) + adam_eps)
    weight = weight - update - learn_rate * decay_rate * weight
    average = ema_rate * average + (1.0 - ema_rate) * weight
    return (weight, moment_one, moment_two, average)


def kto_terms(sq_sums, counts, labels, utility, ref_loss):
    sample_loss = sq_sums / (counts * D)
    signs = 2.0 * labels.astype(jnp.float32) - 1.0
    chosen = jax.nn.sigmoid(signs * kto_beta * (ref_loss - sample_loss))
    loss = -jnp.sum(utility * chosen) / SAMPLES
    dloss = utility * chosen * (1.0 - chosen) * signs * kto_beta / SAMPLES
    sample_coef = loss_scale * 2.0 * dloss / (counts * D)
    return (loss, sample_coef)


def product(left, right, left_dim, right_dim):
    return lax.dot_general(
        left,
        right,
        (((left_dim,), (right_dim,)), ((), ())),
        precision=mixed,
        preferred_element_type=jnp.float32,
    )


def scatter_sum(part, axis, size, groups=None):
    blocks = part.reshape(size, part.shape[0] // size, part.shape[1])
    return jnp.sum(lax.all_to_all(blocks, axis, 0, 0, axis_index_groups=groups), axis=0)


def spread(block, axis, size, groups=None):
    copies = jnp.broadcast_to(block[None], (size,) + block.shape)
    return lax.all_to_all(copies, axis, 0, 0, axis_index_groups=groups)


def y_sum(part):
    return scatter_sum(part, "inp", 4, QUADS)


def far_sum(quarter):
    return quarter + lax.ppermute(quarter, "inp", FAR_HALF)


def y_gather(block):
    every = spread(block, "inp", 4, QUADS)
    return every.reshape(4 * block.shape[0], block.shape[1])


def queue_gather(shard, after=None):
    folded = lax.all_gather(shard, "tok", axis=0, tiled=False, axis_index_groups=[list(FOLD)])
    if after is not None:
        folded, after = lax.optimization_barrier((folded, after))
    return ring_order(folded).reshape(8 * shard.shape[0], shard.shape[1]), after


def fold_rows(full):
    pairs = full.reshape(4, 2, full.shape[0] // 8, full.shape[1])
    folded = jnp.concatenate([pairs[:, 0], jnp.flip(pairs[:, 1], axis=0)], axis=0)
    return folded.reshape(full.shape)


def queue_scatter(folded):
    return lax.psum_scatter(
        folded, "tok", scatter_dimension=0, tiled=True, axis_index_groups=[list(FOLD)]
    )


def ring_order(folded):
    pairs = jnp.stack([folded[:4], jnp.flip(folded[4:], axis=0)], axis=1)
    return pairs.reshape((8,) + folded.shape[1:])


def core_gather(shard, split):
    small = spread(shard[split:], "tok", 8)
    large = lax.all_gather(
        shard[:split], "tok", axis=0, tiled=False, axis_index_groups=[list(FOLD)]
    )
    every = jnp.concatenate([ring_order(large), small], axis=1)
    return every.reshape(8 * shard.shape[0], shard.shape[1])


def half_pair(shard):
    upper = lax.axis_index("tok") >= 4
    other = lax.ppermute(shard, "tok", FAR_HALF)
    return jnp.concatenate([jnp.where(upper, other, shard), jnp.where(upper, shard, other)])


def quad_columns(tokens, sample_ids):
    blocks = jnp.transpose(tokens.reshape(16, 2, 4, 48), (2, 0, 1, 3)).reshape(4, 16, 96)
    id_lanes = jnp.broadcast_to(sample_ids.astype(jnp.float32)[None, :, None], (4, 16, 32))
    blocks = jnp.concatenate([blocks, id_lanes], axis=2)
    copies = jnp.broadcast_to(blocks[None], (8, 4, 16, 128)).reshape(32, 16, 128)
    every = lax.all_to_all(copies, ("hid", "tok"), 0, 0, axis_index_groups=HID_QUADS)
    every = every.reshape(4, 2, 4, 16, 128)
    return jnp.transpose(every, (0, 2, 1, 3, 4)).reshape(512, 128)


def quad_rows(block):
    near = spread(block, "tok", 4, QUADS).reshape(128, 768)
    return spread(near, "inp", 4, QUADS).reshape(512, 768)


def half_sum(pair):
    upper = lax.axis_index("tok") >= 4
    rows = pair.shape[0] // 2
    keep = jnp.where(upper, pair[rows:], pair[:rows])
    send = jnp.where(upper, pair[:rows], pair[rows:])
    other = lax.ppermute(send, "tok", FAR_HALF)
    return keep + other


def on_device(
    tokens,
    targets,
    sample_ids,
    labels,
    utility,
    ref_loss,
    w_in,
    w_out,
    m_in,
    m_out,
    v_in,
    v_out,
    e_in,
    e_out,
):
    w_in_pair = half_pair(w_in)
    table = quad_columns(tokens, sample_ids)
    columns = table[:, :96]
    quad_ids = table[:, 96].reshape(4, 4, 32)
    own_quad = lax.rem(lax.axis_index("tok"), 4)
    all_ids = lax.dynamic_index_in_dim(quad_ids, own_quad, axis=1, keepdims=False)
    all_ids = all_ids.reshape(-1).astype(jnp.int32)
    onehot = (all_ids[:, None] == jnp.arange(SAMPLES, dtype=jnp.int32)[None, :]).astype(
        jnp.float32
    )
    quad_part = y_sum(product(columns, w_in_pair, 1, 0))
    hidden = far_sum(scatter_sum(quad_part, "tok", 4, QUADS))
    active_rows, slope_rows = gelu_parts(hidden)
    active = y_gather(active_rows)
    w_out_block, active = queue_gather(w_out, active)

    output = scatter_sum(product(active, w_out_block, 1, 0), "hid", 8)
    error = spread(output - targets, "hid", 8).reshape(128, 384)
    token_sq = jnp.sum(error * error, axis=1)
    local_sq = jnp.sum(token_sq[:, None] * onehot, axis=0)
    leading = lax.axis_index("inp") == 0
    local_counts = jnp.sum(onehot, axis=0) * jnp.where(leading, 1.0, 0.0)
    stats = jnp.concatenate([local_sq, local_counts, jnp.zeros((96,), jnp.float32)])[None, :]
    d_quarter = y_sum(product(error, w_out_block, 1, 1))
    stats, d_quarter = lax.optimization_barrier((stats, d_quarter))
    stats = jnp.sum(spread(stats, ("inp", "tok"), 64), axis=(0, 1))
    d_active = far_sum(d_quarter)
    loss, sample_coef = kto_terms(
        stats[:SAMPLES], stats[SAMPLES : 2 * SAMPLES], labels, utility, ref_loss
    )
    coef = jnp.sum(onehot * sample_coef[None, :], axis=1)[:, None]
    own_rows = lax.rem(lax.axis_index("inp"), 4) * 32
    own_coef = lax.dynamic_slice(coef, (own_rows, 0), (32, 1))

    grad_fold = fold_rows(product(active, error * coef, 0, 0))
    d_rows = d_active * own_coef * slope_rows
    grad_fold, d_rows = lax.optimization_barrier((grad_fold, d_rows))
    grad_out = queue_scatter(grad_fold)
    grad_in = half_sum(product(columns, quad_rows(d_rows), 0, 0))

    weight_out, new_m_out, new_v_out, new_e_out = adamw(w_out, m_out, v_out, e_out, grad_out)
    new_w_out, _ = queue_gather(weight_out)
    weight_in, new_m_in, new_v_in, new_e_in = adamw(w_in, m_in, v_in, e_in, grad_in)
    new_w_in = core_gather(weight_in, 40)
    return (
        loss,
        new_w_in,
        new_w_out,
        new_m_in,
        new_m_out,
        new_v_in,
        new_v_out,
        new_e_in,
        new_e_out,
    )


def solution(mesh):
    in_specs = (
        P(("tok", "hid"), "inp"),
        P(("tok", "hid"), "inp"),
        P(("tok", "hid")),
        P(),
        P(),
        P(),
        P(("inp", "tok"), "hid"),
        P(("hid", "tok"), "inp"),
        P(("inp", "tok"), "hid"),
        P(("hid", "tok"), "inp"),
        P(("inp", "tok"), "hid"),
        P(("hid", "tok"), "inp"),
        P(("inp", "tok"), "hid"),
        P(("hid", "tok"), "inp"),
    )
    out_specs = (
        P(),
        P("inp", "hid"),
        P("hid", "inp"),
        P(("inp", "tok"), "hid"),
        P(("hid", "tok"), "inp"),
        P(("inp", "tok"), "hid"),
        P(("hid", "tok"), "inp"),
        P(("inp", "tok"), "hid"),
        P(("hid", "tok"), "inp"),
    )
    return jax.shard_map(
        on_device, mesh=mesh, in_specs=in_specs, out_specs=out_specs, check_vma=False
    )
```

```python
import jax
import jax.numpy as jnp
from jax import lax
from jax.sharding import PartitionSpec as P


D = 3072
SAMPLES = 16


mixed = lax.Precision.HIGH
gelu_c = 0.7978845608028654
gelu_k = 0.044715
kto_beta = 4.0
loss_scale = 1048576.0
beta_one = 0.9
beta_two = 0.95
adam_eps = 1e-08
learn_rate = 0.001
decay_rate = 0.1
ema_rate = 0.99
bias_one = 1.0 - 0.9**10
bias_two = 1.0 - 0.95**10


QUADS = [[0, 1, 2, 3], [4, 5, 6, 7]]
FAR_HALF = [(i, (i + 4) % 8) for i in range(8)]
FOLD = (0, 2, 4, 6, 7, 5, 3, 1)


def gelu_parts(hidden):
    inner = gelu_c * (hidden + gelu_k * hidden * hidden * hidden)
    tangent = jnp.tanh(inner)
    active = 0.5 * hidden * (1.0 + tangent)
    slope = 0.5 * (1.0 + tangent) + 0.5 * hidden * (1.0 - tangent * tangent) * gelu_c * (
        1.0 + 3.0 * gelu_k * hidden * hidden
    )
    return (active, slope)


def adamw(weight, moment_one, moment_two, average, gradient):
    moment_one = beta_one * moment_one + (1.0 - beta_one) * gradient
    moment_two = beta_two * moment_two + (1.0 - beta_two) * gradient * gradient
    update = learn_rate * (moment_one / bias_one) / (jnp.sqrt(moment_two / bias_two) + adam_eps)
    weight = weight - update - learn_rate * decay_rate * weight
    average = ema_rate * average + (1.0 - ema_rate) * weight
    return (weight, moment_one, moment_two, average)


def kto_terms(sq_sums, counts, labels, utility, ref_loss):
    sample_loss = sq_sums / (counts * D)
    signs = 2.0 * labels.astype(jnp.float32) - 1.0
    chosen = jax.nn.sigmoid(signs * kto_beta * (ref_loss - sample_loss))
    loss = -jnp.sum(utility * chosen) / SAMPLES
    dloss = utility * chosen * (1.0 - chosen) * signs * kto_beta / SAMPLES
    sample_coef = loss_scale * 2.0 * dloss / (counts * D)
    return (loss, sample_coef)


def product(left, right, left_dim, right_dim):
    return lax.dot_general(
        left,
        right,
        (((left_dim,), (right_dim,)), ((), ())),
        precision=mixed,
        preferred_element_type=jnp.float32,
    )


def scatter_sum(part, axis, size, groups=None):
    blocks = part.reshape(size, part.shape[0] // size, part.shape[1])
    return jnp.sum(lax.all_to_all(blocks, axis, 0, 0, axis_index_groups=groups), axis=0)


def spread(block, axis, size, groups=None):
    copies = jnp.broadcast_to(block[None], (size,) + block.shape)
    return lax.all_to_all(copies, axis, 0, 0, axis_index_groups=groups)


def y_sum(part):
    return scatter_sum(part, "inp", 4, QUADS)


def y_sum_hops(part):
    blocks = part.reshape(4, part.shape[0] // 4, part.shape[1])
    y = lax.rem(lax.axis_index("inp"), 4)
    total = lax.dynamic_index_in_dim(blocks, y, axis=0, keepdims=False)
    for step in (1, 3, 2):
        sent = lax.dynamic_index_in_dim(blocks, lax.rem(y + step, 4), axis=0, keepdims=False)
        pairs = [(i, (i // 4) * 4 + (i % 4 + step) % 4) for i in range(8)]
        total = total + lax.ppermute(sent, "inp", pairs)
    return total


def far_sum(quarter):
    return quarter + lax.ppermute(quarter, "inp", FAR_HALF)


def y_gather(block):
    every = spread(block, "inp", 4, QUADS)
    return every.reshape(4 * block.shape[0], block.shape[1])


def queue_gather(shard, after=None):
    folded = lax.all_gather(shard, "tok", axis=0, tiled=False, axis_index_groups=[list(FOLD)])
    if after is not None:
        folded, after = lax.optimization_barrier((folded, after))
    return ring_order(folded).reshape(8 * shard.shape[0], shard.shape[1]), after


def fold_rows(full):
    pairs = full.reshape(4, 2, full.shape[0] // 8, full.shape[1])
    folded = jnp.concatenate([pairs[:, 0], jnp.flip(pairs[:, 1], axis=0)], axis=0)
    return folded.reshape(full.shape)


def queue_scatter(folded):
    return lax.psum_scatter(
        folded, "tok", scatter_dimension=0, tiled=True, axis_index_groups=[list(FOLD)]
    )


def ring_order(folded):
    pairs = jnp.stack([folded[:4], jnp.flip(folded[4:], axis=0)], axis=1)
    return pairs.reshape((8,) + folded.shape[1:])


def core_gather(shard, split):
    small = spread(shard[split:], "tok", 8)
    large = lax.all_gather(
        shard[:split], "tok", axis=0, tiled=False, axis_index_groups=[list(FOLD)]
    )
    every = jnp.concatenate([ring_order(large), small], axis=1)
    return every.reshape(8 * shard.shape[0], shard.shape[1])


def half_pair(shard):
    upper = lax.axis_index("tok") >= 4
    other = lax.ppermute(shard, "tok", FAR_HALF)
    return jnp.concatenate([jnp.where(upper, other, shard), jnp.where(upper, shard, other)])


def quad_columns(tokens, sample_ids):
    blocks = jnp.transpose(tokens.reshape(16, 2, 4, 48), (2, 0, 1, 3)).reshape(4, 16, 96)
    id_lanes = jnp.broadcast_to(sample_ids.astype(jnp.float32)[None, :, None], (4, 16, 32))
    blocks = jnp.concatenate([blocks, id_lanes], axis=2)
    near = lax.all_to_all(blocks, "tok", 0, 0, axis_index_groups=QUADS)
    every = spread(near, "hid", 8).reshape(4, 2, 4, 16, 128)
    return jnp.transpose(every, (0, 2, 1, 3, 4)).reshape(512, 128)


def quad_rows(block):
    near = spread(block, "tok", 4, QUADS).reshape(128, 768)
    return spread(near, "inp", 4, QUADS).reshape(512, 768)


def half_sum(pair, partner):
    upper = lax.axis_index("tok") >= 4
    rows = pair.shape[0] // 2
    keep = jnp.where(upper, pair[rows:], pair[:rows])
    send = jnp.where(upper, pair[:rows], pair[rows:])
    keep, partner = lax.optimization_barrier((keep, partner))
    other = lax.ppermute(send, "tok", FAR_HALF)
    return keep + other, partner


def on_device(
    tokens,
    targets,
    sample_ids,
    labels,
    utility,
    ref_loss,
    w_in,
    w_out,
    m_in,
    m_out,
    v_in,
    v_out,
    e_in,
    e_out,
):
    w_in_pair = half_pair(w_in)
    table = quad_columns(tokens, sample_ids)
    columns = table[:, :96]
    quad_ids = table[:, 96].reshape(4, 4, 32)
    own_quad = lax.rem(lax.axis_index("tok"), 4)
    all_ids = lax.dynamic_index_in_dim(quad_ids, own_quad, axis=1, keepdims=False)
    all_ids = all_ids.reshape(-1).astype(jnp.int32)
    onehot = (all_ids[:, None] == jnp.arange(SAMPLES, dtype=jnp.int32)[None, :]).astype(
        jnp.float32
    )
    quad_part = y_sum(product(columns, w_in_pair, 1, 0))
    hidden = far_sum(scatter_sum(quad_part, "tok", 4, QUADS))
    active_rows, slope_rows = gelu_parts(hidden)
    active = y_gather(active_rows)
    w_out_block, active = queue_gather(w_out, active)

    output = scatter_sum(product(active, w_out_block, 1, 0), "hid", 8)
    error = spread(output - targets, "hid", 8).reshape(128, 384)
    token_sq = jnp.sum(error * error, axis=1)
    local_sq = jnp.sum(token_sq[:, None] * onehot, axis=0)
    leading = lax.axis_index("inp") == 0
    local_counts = jnp.sum(onehot, axis=0) * jnp.where(leading, 1.0, 0.0)
    stats = jnp.concatenate([local_sq, local_counts, jnp.zeros((96,), jnp.float32)])[None, :]
    stats = spread(stats, ("inp", "tok"), 64)
    stats = jnp.sum(stats, axis=(0, 1))
    d_quarter = y_sum_hops(product(error, w_out_block, 1, 1))
    loss, sample_coef = kto_terms(
        stats[:SAMPLES], stats[SAMPLES : 2 * SAMPLES], labels, utility, ref_loss
    )
    coef = jnp.sum(onehot * sample_coef[None, :], axis=1)[:, None]
    own_rows = lax.rem(lax.axis_index("inp"), 4) * 32
    own_coef = lax.dynamic_slice(coef, (own_rows, 0), (32, 1))

    grad_fold = fold_rows(product(active, error * coef, 0, 0))
    grad_fold, d_quarter = lax.optimization_barrier((grad_fold, d_quarter))
    grad_out = queue_scatter(grad_fold)
    d_rows = far_sum(d_quarter) * own_coef * slope_rows
    grad_in, grad_out = half_sum(product(columns, quad_rows(d_rows), 0, 0), grad_out)

    weight_out, new_m_out, new_v_out, new_e_out = adamw(w_out, m_out, v_out, e_out, grad_out)
    new_w_out, _ = queue_gather(weight_out)
    weight_in, new_m_in, new_v_in, new_e_in = adamw(w_in, m_in, v_in, e_in, grad_in)
    new_w_in = core_gather(weight_in, 40)
    return (
        loss,
        new_w_in,
        new_w_out,
        new_m_in,
        new_m_out,
        new_v_in,
        new_v_out,
        new_e_in,
        new_e_out,
    )


def solution(mesh):
    in_specs = (
        P(("tok", "hid"), "inp"),
        P(("tok", "hid"), "inp"),
        P(("tok", "hid")),
        P(),
        P(),
        P(),
        P(("inp", "tok"), "hid"),
        P(("hid", "tok"), "inp"),
        P(("inp", "tok"), "hid"),
        P(("hid", "tok"), "inp"),
        P(("inp", "tok"), "hid"),
        P(("hid", "tok"), "inp"),
        P(("inp", "tok"), "hid"),
        P(("hid", "tok"), "inp"),
    )
    out_specs = (
        P(),
        P("inp", "hid"),
        P("hid", "inp"),
        P(("inp", "tok"), "hid"),
        P(("hid", "tok"), "inp"),
        P(("inp", "tok"), "hid"),
        P(("hid", "tok"), "inp"),
        P(("inp", "tok"), "hid"),
        P(("hid", "tok"), "inp"),
    )
    return jax.shard_map(
        on_device, mesh=mesh, in_specs=in_specs, out_specs=out_specs, check_vma=False
    )
```

```python
import jax
import jax.numpy as jnp
from jax import lax
from jax.sharding import PartitionSpec as P


D = 3072
SAMPLES = 16


mixed = lax.Precision.HIGH
gelu_c = 0.7978845608028654
gelu_k = 0.044715
kto_beta = 4.0
loss_scale = 1048576.0
beta_one = 0.9
beta_two = 0.95
adam_eps = 1e-08
learn_rate = 0.001
decay_rate = 0.1
ema_rate = 0.99
bias_one = 1.0 - 0.9**10
bias_two = 1.0 - 0.95**10


QUADS = [[0, 1, 2, 3], [4, 5, 6, 7]]
FAR_HALF = [(i, (i + 4) % 8) for i in range(8)]
FOLD = (0, 2, 4, 6, 7, 5, 3, 1)


def gelu_parts(hidden):
    inner = gelu_c * (hidden + gelu_k * hidden * hidden * hidden)
    tangent = jnp.tanh(inner)
    active = 0.5 * hidden * (1.0 + tangent)
    slope = 0.5 * (1.0 + tangent) + 0.5 * hidden * (1.0 - tangent * tangent) * gelu_c * (
        1.0 + 3.0 * gelu_k * hidden * hidden
    )
    return (active, slope)


def adamw(weight, moment_one, moment_two, average, gradient):
    moment_one = beta_one * moment_one + (1.0 - beta_one) * gradient
    moment_two = beta_two * moment_two + (1.0 - beta_two) * gradient * gradient
    update = learn_rate * (moment_one / bias_one) / (jnp.sqrt(moment_two / bias_two) + adam_eps)
    weight = weight - update - learn_rate * decay_rate * weight
    average = ema_rate * average + (1.0 - ema_rate) * weight
    return (weight, moment_one, moment_two, average)


def kto_terms(sq_sums, counts, labels, utility, ref_loss):
    sample_loss = sq_sums / (counts * D)
    signs = 2.0 * labels.astype(jnp.float32) - 1.0
    chosen = jax.nn.sigmoid(signs * kto_beta * (ref_loss - sample_loss))
    loss = -jnp.sum(utility * chosen) / SAMPLES
    dloss = utility * chosen * (1.0 - chosen) * signs * kto_beta / SAMPLES
    sample_coef = loss_scale * 2.0 * dloss / (counts * D)
    return (loss, sample_coef)


def product(left, right, left_dim, right_dim):
    return lax.dot_general(
        left,
        right,
        (((left_dim,), (right_dim,)), ((), ())),
        precision=mixed,
        preferred_element_type=jnp.float32,
    )


def scatter_sum(part, axis, size, groups=None):
    blocks = part.reshape(size, part.shape[0] // size, part.shape[1])
    return jnp.sum(lax.all_to_all(blocks, axis, 0, 0, axis_index_groups=groups), axis=0)


def spread(block, axis, size, groups=None):
    copies = jnp.broadcast_to(block[None], (size,) + block.shape)
    return lax.all_to_all(copies, axis, 0, 0, axis_index_groups=groups)


def y_sum(part):
    return scatter_sum(part, "inp", 4, QUADS)


def y_sum_hops(part):
    blocks = part.reshape(4, part.shape[0] // 4, part.shape[1])
    y = lax.rem(lax.axis_index("inp"), 4)
    total = lax.dynamic_index_in_dim(blocks, y, axis=0, keepdims=False)
    for step in (1, 3, 2):
        sent = lax.dynamic_index_in_dim(blocks, lax.rem(y + step, 4), axis=0, keepdims=False)
        pairs = [(i, (i // 4) * 4 + (i % 4 + step) % 4) for i in range(8)]
        total = total + lax.ppermute(sent, "inp", pairs)
    return total


def far_sum(quarter):
    return quarter + lax.ppermute(quarter, "inp", FAR_HALF)


def y_gather(block):
    every = spread(block, "inp", 4, QUADS)
    return every.reshape(4 * block.shape[0], block.shape[1])


def queue_gather(shard, after=None):
    folded = lax.all_gather(shard, "tok", axis=0, tiled=False, axis_index_groups=[list(FOLD)])
    if after is not None:
        folded, after = lax.optimization_barrier((folded, after))
    return ring_order(folded).reshape(8 * shard.shape[0], shard.shape[1]), after


def fold_rows(full):
    pairs = full.reshape(4, 2, full.shape[0] // 8, full.shape[1])
    folded = jnp.concatenate([pairs[:, 0], jnp.flip(pairs[:, 1], axis=0)], axis=0)
    return folded.reshape(full.shape)


def queue_scatter(folded):
    return lax.psum_scatter(
        folded, "tok", scatter_dimension=0, tiled=True, axis_index_groups=[list(FOLD)]
    )


def ring_order(folded):
    pairs = jnp.stack([folded[:4], jnp.flip(folded[4:], axis=0)], axis=1)
    return pairs.reshape((8,) + folded.shape[1:])


def core_gather(shard, split):
    small = spread(shard[split:], "tok", 8)
    large = lax.all_gather(
        shard[:split], "tok", axis=0, tiled=False, axis_index_groups=[list(FOLD)]
    )
    every = jnp.concatenate([ring_order(large), small], axis=1)
    return every.reshape(8 * shard.shape[0], shard.shape[1])


def half_pair(shard):
    upper = lax.axis_index("tok") >= 4
    other = lax.ppermute(shard, "tok", FAR_HALF)
    return jnp.concatenate([jnp.where(upper, other, shard), jnp.where(upper, shard, other)])


def quad_columns(tokens, sample_ids):
    blocks = jnp.transpose(tokens.reshape(16, 2, 4, 48), (2, 0, 1, 3)).reshape(4, 16, 96)
    id_lanes = jnp.broadcast_to(sample_ids.astype(jnp.float32)[None, :, None], (4, 16, 32))
    blocks = jnp.concatenate([blocks, id_lanes], axis=2)
    near = lax.all_to_all(blocks, "tok", 0, 0, axis_index_groups=QUADS)
    every = spread(near, "hid", 8).reshape(4, 2, 4, 16, 128)
    return jnp.transpose(every, (0, 2, 1, 3, 4)).reshape(512, 128)


def quad_rows(block):
    near = spread(block, "tok", 4, QUADS).reshape(128, 768)
    return spread(near, "inp", 4, QUADS).reshape(512, 768)


def half_sum(pair):
    upper = lax.axis_index("tok") >= 4
    rows = pair.shape[0] // 2
    keep = jnp.where(upper, pair[rows:], pair[:rows])
    send = jnp.where(upper, pair[:rows], pair[rows:])
    other = lax.ppermute(send, "tok", FAR_HALF)
    return keep + other


def on_device(
    tokens,
    targets,
    sample_ids,
    labels,
    utility,
    ref_loss,
    w_in,
    w_out,
    m_in,
    m_out,
    v_in,
    v_out,
    e_in,
    e_out,
):
    w_in_pair = half_pair(w_in)
    table = quad_columns(tokens, sample_ids)
    columns = table[:, :96]
    quad_ids = table[:, 96].reshape(4, 4, 32)
    own_quad = lax.rem(lax.axis_index("tok"), 4)
    all_ids = lax.dynamic_index_in_dim(quad_ids, own_quad, axis=1, keepdims=False)
    all_ids = all_ids.reshape(-1).astype(jnp.int32)
    onehot = (all_ids[:, None] == jnp.arange(SAMPLES, dtype=jnp.int32)[None, :]).astype(
        jnp.float32
    )
    quad_part = y_sum(product(columns, w_in_pair, 1, 0))
    hidden = far_sum(scatter_sum(quad_part, "tok", 4, QUADS))
    active_rows, slope_rows = gelu_parts(hidden)
    active = y_gather(active_rows)
    w_out_block, active = queue_gather(w_out, active)

    output = scatter_sum(product(active, w_out_block, 1, 0), "hid", 8)
    error = spread(output - targets, "hid", 8).reshape(128, 384)
    token_sq = jnp.sum(error * error, axis=1)
    local_sq = jnp.sum(token_sq[:, None] * onehot, axis=0)
    leading = lax.axis_index("inp") == 0
    local_counts = jnp.sum(onehot, axis=0) * jnp.where(leading, 1.0, 0.0)
    stats = jnp.concatenate([local_sq, local_counts, jnp.zeros((96,), jnp.float32)])[None, :]
    stats = spread(stats, ("inp", "tok"), 64)
    stats = jnp.sum(stats, axis=(0, 1))
    d_quarter = y_sum_hops(product(error, w_out_block, 1, 1))
    loss, sample_coef = kto_terms(
        stats[:SAMPLES], stats[SAMPLES : 2 * SAMPLES], labels, utility, ref_loss
    )
    coef = jnp.sum(onehot * sample_coef[None, :], axis=1)[:, None]
    own_rows = lax.rem(lax.axis_index("inp"), 4) * 32
    own_coef = lax.dynamic_slice(coef, (own_rows, 0), (32, 1))

    grad_fold = fold_rows(product(active, error * coef, 0, 0))
    grad_fold, d_quarter = lax.optimization_barrier((grad_fold, d_quarter))
    grad_out = queue_scatter(grad_fold)
    d_rows = far_sum(d_quarter) * own_coef * slope_rows
    d_hidden, grad_out = lax.optimization_barrier((quad_rows(d_rows), grad_out))
    grad_in = half_sum(product(columns, d_hidden, 0, 0))

    weight_out, new_m_out, new_v_out, new_e_out = adamw(w_out, m_out, v_out, e_out, grad_out)
    new_w_out = core_gather(weight_out, 80)
    weight_in, new_m_in, new_v_in, new_e_in = adamw(w_in, m_in, v_in, e_in, grad_in)
    new_w_in, _ = queue_gather(weight_in)
    return (
        loss,
        new_w_in,
        new_w_out,
        new_m_in,
        new_m_out,
        new_v_in,
        new_v_out,
        new_e_in,
        new_e_out,
    )


def solution(mesh):
    in_specs = (
        P(("tok", "hid"), "inp"),
        P(("tok", "hid"), "inp"),
        P(("tok", "hid")),
        P(),
        P(),
        P(),
        P(("inp", "tok"), "hid"),
        P(("hid", "tok"), "inp"),
        P(("inp", "tok"), "hid"),
        P(("hid", "tok"), "inp"),
        P(("inp", "tok"), "hid"),
        P(("hid", "tok"), "inp"),
        P(("inp", "tok"), "hid"),
        P(("hid", "tok"), "inp"),
    )
    out_specs = (
        P(),
        P("inp", "hid"),
        P("hid", "inp"),
        P(("inp", "tok"), "hid"),
        P(("hid", "tok"), "inp"),
        P(("inp", "tok"), "hid"),
        P(("hid", "tok"), "inp"),
        P(("inp", "tok"), "hid"),
        P(("hid", "tok"), "inp"),
    )
    return jax.shard_map(
        on_device, mesh=mesh, in_specs=in_specs, out_specs=out_specs, check_vma=False
    )
```
